128 devices in a mesh: group: 16 (over y, z_hi, core), ctx: 8 (over x, z_lo).
Axes of the slice: x: 4, y: 4, z: 4 (z_hi: 2, z_lo: 2; z = z_hi * 2 + z_lo), core: 2. Of those that a mesh axis runs over, the one named last changes fastest.
Arguments:
- query: bfloat16 [16, 4, 32, 8192], P('group', None, None, 'ctx'), may hold values from -160 to 160
- cache_keys: bfloat16 [16, 4, 4096, 1024], P('group', None, 'ctx'), may hold values from -6 to 6
- cache_values: bfloat16 [16, 4, 4096, 1024], P('group', None, 'ctx'), may hold values from -6 to 6
- new_keys: bfloat16 [16, 4, 32, 1024], P('group', None, 'ctx'), may hold values from -6 to 6
- new_values: bfloat16 [16, 4, 32, 1024], P('group', None, 'ctx'), may hold values from -6 to 6
- masks: int32 [3], replicated, may hold values from 1 to 15
- movers: int32 [3, 16], replicated, may hold values from 0 to 3
- block_lists: int32 [3, 16, 4], replicated, may hold values from 0 to 3, as said below
- lengths: int32 [16, 4], replicated, may hold values from 1 to 4096
Outputs:
- attended: bfloat16 [16, 4, 32, 8192], P('group', None, None, 'ctx')
- keys_after: bfloat16 [16, 4, 4096, 1024], P('group', None, 'ctx')
- values_after: bfloat16 [16, 4, 4096, 1024], P('group', None, 'ctx')
The draws below stay inside these ranges and needn't reach their ends.
Inputs may be any that keep to these rules, and one draw needn't show every extreme that they name: `block_lists`: each row is a permutation of the 4 blocks.
All inputs are finite; a program needn't handle non-finite values.
Results may differ from the reference program's by a relative error of at most 0.005.
Values may be sent and summed in bfloat16 or wider, within the bound.
A program may use at most 192 MiB of HBM per device.

```python
import jax
import jax.numpy as jnp
from jax import lax

QH = 64
KVH = 8
HD = 128
R = 4
NEW = 32
MATCHINGS = 3
BLOCK = 128
GQ = 8
NB = 4
MOVE = 4
LEN = 4096
GROUPS = 16
N_GROUP = 16
N_CTX = 8


def anchors(key):
    base = jax.random.fold_in(key, 11)
    parts = jax.random.split(base, 4)
    lead_levels = jax.random.randint(parts[0], (KVH, HD), -32, 33).astype(jnp.float32)
    lead_nudges = jax.random.randint(parts[1], (KVH, HD), -1, 2).astype(jnp.float32)
    side_levels = jax.random.randint(parts[2], (KVH, HD), -24, 25).astype(jnp.float32)
    side_nudges = jax.random.randint(parts[3], (KVH, HD), -1, 2).astype(jnp.float32)
    leading = lead_levels / 16.0
    nearby = (lead_levels + lead_nudges) / 16.0
    side = side_levels / 16.0
    side_near = (side_levels + side_nudges) / 16.0
    return (leading, nearby, side, side_near)


def paired_draw(key):
    leading, nearby, side, side_near = anchors(key)
    base = jax.random.fold_in(key, 7)
    parts = jax.random.split(base, 7)
    fresh = jnp.clip(jax.random.normal(parts[0], (GROUPS, R, NEW, KVH, HD), jnp.float32), -6.0, 6.0)
    lead_rows = jnp.broadcast_to(leading[None, None, None], (GROUPS, R, 1, KVH, HD))
    near_rows = jnp.broadcast_to(nearby[None, None, None], (GROUPS, R, 1, KVH, HD))
    fresh = jnp.concatenate([lead_rows, near_rows, fresh[:, :, 2:]], axis=2)
    asked = jnp.clip(2.0 * jax.random.normal(parts[1], (GROUPS, R, NEW, KVH, QH // KVH, HD), jnp.float32), -12.0, 12.0)
    strength = 4.0 * jax.random.randint(parts[3], (GROUPS, R, NEW, KVH, QH // KVH, 1), 3, 7).astype(jnp.float32)
    later = (jnp.arange(NEW) >= 1)[None, None, :, None, None, None]
    picked = jnp.logical_and(jax.random.bernoulli(parts[4], 0.06, (GROUPS, R, NEW, KVH, QH // KVH, 1)), later)
    asked = jnp.where(picked, strength * leading[None, None, None, :, None, :], asked)
    side_strength = 4.0 * jax.random.randint(parts[5], (GROUPS, R, NEW, KVH, QH // KVH, 1), 5, 8).astype(jnp.float32)
    side_picked = jnp.logical_and(jax.random.bernoulli(parts[6], 0.06, (GROUPS, R, NEW, KVH, QH // KVH, 1)), jnp.logical_not(picked))
    asked = jnp.where(side_picked, side_strength * side[None, None, None, :, None, :], asked)
    return (asked.reshape(GROUPS, R, NEW, QH * HD), fresh.reshape(GROUPS, R, NEW, KVH * HD))


def draw_query(key, part):
    return paired_draw(key)[0].astype(jnp.bfloat16)


def draw_new_keys(key, part):
    return paired_draw(key)[1].astype(jnp.bfloat16)


def draw_cache_keys(key, part):
    leading, nearby, side, side_near = anchors(key)
    inner = jax.random.fold_in(key, 13)
    rest = jnp.clip(jax.random.normal(inner, (GROUPS, R, LEN, KVH, HD), jnp.float32), -6.0, 6.0)
    within = (jnp.arange(LEN, dtype=jnp.int32) % BLOCK)[None, None, :, None, None]
    rest = jnp.where(within == 2, side_near[None, None, None], rest)
    rest = jnp.where(within == 1, side[None, None, None], rest)
    rest = jnp.where(within == 0, leading[None, None, None], rest)
    return rest.reshape(GROUPS, R, LEN, KVH * HD).astype(jnp.bfloat16)


def draw_block_lists(key, part):
    scores = jax.random.randint(jax.random.fold_in(key, 3), (MATCHINGS, GROUPS, NB), 0, 1 << 20) * NB
    scores = scores + jnp.arange(NB, dtype=jnp.int32)
    order = jnp.argsort(scores, axis=-1)
    return order[..., :MOVE].astype(jnp.int32)


def plant(array, own_key, least, high):
    spot = [jax.random.randint(jax.random.fold_in(own_key, axis), (), 0, length) for axis, length in enumerate(array.shape)]
    widest = array.shape.index(max(array.shape))
    neighbour = spot[:widest] + [(spot[widest] + 1) % array.shape[widest]] + spot[widest + 1:]
    return array.at[tuple(spot)].set(least).at[tuple(neighbour)].set(high)


def block_scale(key, shape, cuts, low, high):
    level, own = 1.0, jax.random.fold_in(key, 6)
    for dim, blocks in cuts:
        draws = jnp.exp(jax.random.uniform(jax.random.fold_in(own, dim), (blocks,), jnp.float32, low / len(cuts), high / len(cuts)))
        level = level * jnp.repeat(draws, shape[dim] // blocks).reshape([-1 if axis == dim else 1 for axis in range(len(shape))])
    return level


def gaussian(own_key, dims, deviation, bound, shards=(), kind=jnp.bfloat16):
    result = jax.random.normal(own_key, dims, jnp.float32) * deviation
    if len(shards) > 0:
        result = block_scale(own_key, dims, shards, -0.22, 0.18) * result
    return jnp.clip(result, min=-bound, max=bound).astype(kind)


def setup_inputs(seed: int = 0) -> dict:
    key_of = jax.random.split(jax.random.key(seed), 10)
    return {
        "query": draw_query(jax.random.fold_in(key_of[9], 71), 0),
        "cache_keys": draw_cache_keys(jax.random.fold_in(key_of[9], 71), 0),
        "cache_values": gaussian(key_of[2], (GROUPS, R, LEN, KVH * HD), 1.0, 6.0, ((0, 16), (2, 8))),
        "new_keys": draw_new_keys(jax.random.fold_in(key_of[9], 71), 0),
        "new_values": gaussian(key_of[4], (GROUPS, R, NEW, KVH * HD), 1.0, 6.0, ((0, 16), (2, 8))),
        "masks": jax.random.randint(key_of[5], (MATCHINGS,), 1, N_GROUP).astype(jnp.int32),
        "movers": plant(jax.random.randint(key_of[6], (MATCHINGS, GROUPS), 0, R), jax.random.fold_in(key_of[6], 1), 0, R - 1).astype(jnp.int32),
        "block_lists": draw_block_lists(jax.random.fold_in(key_of[9], 71), 0),
        "lengths": plant(jax.random.randint(key_of[8], (GROUPS, R), 1, LEN + 1), jax.random.fold_in(key_of[8], 1), 1, LEN).astype(jnp.int32),
    }


def attend_group(args):
    query, keys, values, fresh_keys, fresh_values, counts = args
    scale = 1.0 / (HD ** 0.5)
    heads_q = query.astype(jnp.float32).reshape(R, NEW, KVH, GQ, HD)
    keys_h = keys.astype(jnp.float32).reshape(R, LEN, KVH, HD)
    values_h = values.astype(jnp.float32).reshape(R, LEN, KVH, HD)
    fresh_k = fresh_keys.astype(jnp.float32).reshape(R, NEW, KVH, HD)
    fresh_v = fresh_values.astype(jnp.float32).reshape(R, NEW, KVH, HD)
    older = jnp.einsum('rtkgd,rskd->rkgts', heads_q, keys_h, precision=lax.Precision.HIGHEST) * scale
    newer = jnp.einsum('rtkgd,rskd->rkgts', heads_q, fresh_k, precision=lax.Precision.HIGHEST) * scale
    valid_old = (jnp.arange(LEN, dtype=jnp.int32)[None, :] < counts[:, None])[:, None, None, None, :]
    valid_new = (jnp.arange(NEW, dtype=jnp.int32)[None, :] <= jnp.arange(NEW, dtype=jnp.int32)[:, None])[None, None, None, :, :]
    older = jnp.where(valid_old, older, -jnp.inf)
    newer = jnp.where(valid_new, newer, -jnp.inf)
    top = jnp.maximum(jnp.max(older, axis=-1), jnp.max(newer, axis=-1))
    exp_old = jnp.where(valid_old, jnp.exp(older - top[..., None]), 0.0)
    exp_new = jnp.where(valid_new, jnp.exp(newer - top[..., None]), 0.0)
    total = jnp.sum(exp_old, axis=-1) + jnp.sum(exp_new, axis=-1)
    weight_old = exp_old.astype(jnp.bfloat16).astype(jnp.float32)
    weight_new = exp_new.astype(jnp.bfloat16).astype(jnp.float32)
    summed = jnp.einsum('rkgts,rskd->rtkgd', weight_old, values_h, precision=lax.Precision.HIGHEST)
    summed = summed + jnp.einsum('rkgts,rskd->rtkgd', weight_new, fresh_v, precision=lax.Precision.HIGHEST)
    summed = summed / jnp.transpose(total, (0, 3, 1, 2))[..., None]
    return summed.reshape(R, NEW, QH * HD).astype(jnp.bfloat16)


def reference(query, cache_keys, cache_values, new_keys, new_values, masks, movers, block_lists, lengths):
    every = jnp.arange(GROUPS, dtype=jnp.int32)
    features = KVH * HD
    keys = cache_keys.reshape(GROUPS, R, N_CTX, NB, BLOCK, features)
    values = cache_values.reshape(GROUPS, R, N_CTX, NB, BLOCK, features)
    counts = lengths
    for step in range(MATCHINGS):
        partner = jnp.bitwise_xor(every, masks[step]).astype(jnp.int32)
        slots = movers[step]
        chosen = block_lists[step]
        row_index = every[:, None]
        slot_index = slots[:, None]
        sent_keys = keys[row_index, slot_index, :, chosen]
        sent_values = values[row_index, slot_index, :, chosen]
        keys = keys.at[row_index, slot_index, :, chosen].set(sent_keys[partner])
        values = values.at[row_index, slot_index, :, chosen].set(sent_values[partner])
        counts = counts.at[every, slots].set(counts[partner, slots[partner]])
    keys_after = keys.reshape(GROUPS, R, LEN, features)
    values_after = values.reshape(GROUPS, R, LEN, features)
    attended = lax.map(attend_group, (query, keys_after, values_after, new_keys, new_values, counts))
    return attended, keys_after, values_after
```

```python
import functools
import math

import jax
import jax.numpy as jnp
from jax import lax
from jax.experimental import pallas as pl
from jax.experimental.pallas import tpu as pltpu
from jax.sharding import PartitionSpec as P

HD = 128
NEW = 32
MATCHINGS = 3
BLOCK = 128
GROUPS = 16
WIDTH = 8
SLOTS = 4
SEG = 512
NB = 4
FEATURES = 1024
KVH = 8
GQ = 8
ROWS = GQ * NEW
OWN_NEW = 4
PAD_NEW = 16
MESH = pl.DeviceIdType.MESH
ANY = pl.ANY


def peer_at(place, offset):
    x, z = place // 2, place % 2
    return ((x + offset // 2) % 4) * 2 + (z + offset % 2) % 2


def pack_body(where, keys_ref, values_ref, out_ref):
    out_ref[0, 0] = keys_ref[0]
    out_ref[1, 0] = values_ref[0]


def pack(where, keys, values):
    def spec():
        return pl.BlockSpec((1, BLOCK, FEATURES), lambda j, w: (w[0], w[1 + j], 0))

    return pl.pallas_call(
        pack_body,
        grid_spec=pltpu.PrefetchScalarGridSpec(
            num_scalar_prefetch=1,
            grid=(NB,),
            in_specs=[spec(), spec()],
            out_specs=pl.BlockSpec((2, 1, BLOCK, FEATURES), lambda j, w: (0, j, 0, 0)),
        ),
        out_shape=jax.ShapeDtypeStruct((2, NB, BLOCK, FEATURES), jnp.bfloat16),
        name="pack",
    )(where, keys, values)


def unpack_body(where, arrived_ref, keys_in, values_in, keys_ref, values_ref):
    keys_ref[0] = arrived_ref[0, 0]
    values_ref[0] = arrived_ref[1, 0]


def unpack(where, arrived, keys, values):
    def spec():
        return pl.BlockSpec((1, BLOCK, FEATURES), lambda j, w: (w[0], w[1 + j], 0))

    shape = jax.ShapeDtypeStruct(keys.shape, keys.dtype)
    return pl.pallas_call(
        unpack_body,
        grid_spec=pltpu.PrefetchScalarGridSpec(
            num_scalar_prefetch=1,
            grid=(NB,),
            in_specs=[
                pl.BlockSpec((2, 1, BLOCK, FEATURES), lambda j, w: (0, j, 0, 0)),
                pl.BlockSpec(memory_space=ANY),
                pl.BlockSpec(memory_space=ANY),
            ],
            out_specs=[spec(), spec()],
        ),
        out_shape=[shape, shape],
        input_output_aliases={2: 0, 3: 1},
        name="unpack",
    )(where, arrived, keys, values)


def gather_queries(query):
    parts = [query]
    for offset in range(1, WIDTH):
        route = [(peer_at(me, offset), me) for me in range(WIDTH)]
        parts.append(lax.ppermute(query, "ctx", route))
    return jnp.stack(parts)


def exchange(mask, payload):
    def branch(d):
        route = [(g, g ^ d) for g in range(GROUPS)]
        return lambda block: lax.ppermute(block, "group", route)

    return lax.switch(mask - 1, [branch(d) for d in range(1, GROUPS)], payload)


def attend_body(plan, valid, peers, q_ref, k_ref, v_ref, nk_ref, nv_ref, o_ref, s_ref):
    count = valid[pl.program_id(0)]
    first = peers[WIDTH]
    factor = math.log2(math.e) / math.sqrt(HD)
    q = q_ref[0, 0]
    rows = jnp.concatenate([q[:, g * HD : (g + 1) * HD] for g in range(GQ)], axis=0)
    contract_last = (((1,), (1,)), ((), ()))
    contract_first = (((0,), (0,)), ((), ()))
    older = lax.dot_general(k_ref[0], rows, contract_last, preferred_element_type=jnp.float32)
    newer = lax.dot_general(nk_ref[0], rows, contract_last, preferred_element_type=jnp.float32)
    position = lax.broadcasted_iota(jnp.int32, older.shape, 0)
    valid_old = position < count
    fresh = lax.broadcasted_iota(jnp.int32, newer.shape, 0)
    token = lax.broadcasted_iota(jnp.int32, newer.shape, 1) % NEW
    valid_new = jnp.logical_and(fresh < OWN_NEW, first + fresh <= token)
    older = jnp.where(valid_old, older, -1e30)
    newer = jnp.where(valid_new, newer, -1e30)
    top = jnp.maximum(
        jnp.max(older, axis=0, keepdims=True), jnp.max(newer, axis=0, keepdims=True)
    )
    exp_old = jnp.where(valid_old, jnp.exp2((older - top) * factor), 0.0)
    exp_new = jnp.where(valid_new, jnp.exp2((newer - top) * factor), 0.0)
    total = jnp.sum(exp_old, axis=0, keepdims=True) + jnp.sum(exp_new, axis=0, keepdims=True)
    summed = lax.dot_general(
        v_ref[0], exp_old.astype(jnp.bfloat16), contract_first, preferred_element_type=jnp.float32
    )
    summed += lax.dot_general(
        nv_ref[0], exp_new.astype(jnp.bfloat16), contract_first, preferred_element_type=jnp.float32
    )
    o_ref[0, 0] = summed.astype(jnp.bfloat16)
    row = lax.broadcasted_iota(jnp.int32, (8, ROWS), 0)
    s_ref[0, 0] = jnp.where(row == 0, top, total)


def attend(plan, valid, peers, queries, keys, values, new_keys, new_values):
    n = plan.shape[0]

    def cache():
        return pl.BlockSpec((1, SEG, HD), lambda i, o, p, v, e: (p[i], 0, e[o]))

    def new():
        return pl.BlockSpec((1, PAD_NEW, HD), lambda i, o, p, v, e: (p[i], 0, e[o]))

    return pl.pallas_call(
        attend_body,
        grid_spec=pltpu.PrefetchScalarGridSpec(
            num_scalar_prefetch=3,
            grid=(n, WIDTH),
            in_specs=[
                pl.BlockSpec((1, 1, NEW, GQ * HD), lambda i, o, p, v, e: (o, p[i], 0, 0)),
                cache(),
                cache(),
                new(),
                new(),
            ],
            out_specs=[
                pl.BlockSpec((1, 1, HD, ROWS), lambda i, o, p, v, e: (e[o], i, 0, 0)),
                pl.BlockSpec((1, 1, 8, ROWS), lambda i, o, p, v, e: (e[o], i, 0, 0)),
            ],
        ),
        out_shape=[
            jax.ShapeDtypeStruct((WIDTH, n, HD, ROWS), jnp.bfloat16),
            jax.ShapeDtypeStruct((WIDTH, n, 8, ROWS), jnp.float32),
        ],
        name="attend",
    )(plan, valid, peers, queries, keys, values, new_keys, new_values)


def combine_body(n, o_ref, s_ref, out_ref, o_all, s_all, sem_o, sem_s, arrive_o, arrive_s, local):
    group = lax.axis_index("group")
    place = lax.axis_index("ctx")
    barrier = pltpu.get_barrier_semaphore()
    for offset in range(1, WIDTH):
        pl.semaphore_signal(
            barrier, inc=1, device_id=(group, peer_at(place, offset)), device_id_type=MESH
        )
    own_o = pltpu.make_async_copy(o_ref.at[place], o_all.at[0], local.at[0])
    own_s = pltpu.make_async_copy(s_ref.at[place], s_all.at[0], local.at[1])
    own_o.start()
    own_s.start()
    pl.semaphore_wait(barrier, WIDTH - 1)
    sends = []
    for offset in range(1, WIDTH):
        peer = peer_at(place, offset)
        for src, dst, send, recv in (
            (o_ref, o_all, sem_o, arrive_o),
            (s_ref, s_all, sem_s, arrive_s),
        ):
            copy = pltpu.make_async_remote_copy(
                src_ref=src.at[peer],
                dst_ref=dst.at[offset],
                send_sem=send.at[offset],
                recv_sem=recv.at[offset],
                device_id=(group, peer),
                device_id_type=MESH,
            )
            copy.start()
            sends.append(copy)
    own_o.wait()
    own_s.wait()
    for copy in sends:
        copy.wait()
    factor = math.log2(math.e) / math.sqrt(HD)
    for i in range(n):
        stats = [s_all[offset, i] for offset in range(WIDTH)]
        tops = [part[0:1] for part in stats]
        totals = [part[1:2] for part in stats]
        top = functools.reduce(jnp.maximum, tops)
        scales = [jnp.exp2((part - top) * factor) for part in tops]
        total = sum(a * b for a, b in zip(scales, totals))
        merged = sum(
            o_all[offset, i].astype(jnp.float32) * scales[offset] for offset in range(WIDTH)
        )
        rows = jnp.transpose(merged / total)
        for g in range(GQ):
            out_ref[i, :, g * HD : (g + 1) * HD] = rows[g * NEW : (g + 1) * NEW].astype(
                jnp.bfloat16
            )


def combine(partial, stats):
    n = partial.shape[1]
    dma = pltpu.SemaphoreType.DMA((WIDTH,))
    return pl.pallas_call(
        functools.partial(combine_body, n),
        in_specs=[pl.BlockSpec(memory_space=ANY)] * 2,
        out_specs=pl.BlockSpec(memory_space=pltpu.VMEM),
        out_shape=jax.ShapeDtypeStruct((n, NEW, GQ * HD), jnp.bfloat16),
        scratch_shapes=[
            pltpu.VMEM((WIDTH, n, HD, ROWS), jnp.bfloat16),
            pltpu.VMEM((WIDTH, n, 8, ROWS), jnp.float32),
            dma,
            dma,
            dma,
            dma,
            pltpu.SemaphoreType.DMA((2,)),
        ],
        compiler_params=pltpu.CompilerParams(collective_id=0, has_side_effects=True),
        name="combine",
    )(partial, stats)


def shards(
    query, cache_keys, cache_values, new_keys, new_values, masks, movers, block_lists, lengths
):
    here = lax.axis_index("group")
    place = lax.axis_index("ctx")
    keys = cache_keys[0]
    values = cache_values[0]
    every = jnp.arange(GROUPS, dtype=jnp.int32)
    counts = lengths
    queries = gather_queries(query[0])
    for step in range(MATCHINGS):
        partner = jnp.bitwise_xor(every, masks[step])
        slots = movers[step]
        counts = counts.at[every, slots].set(counts[partner, slots[partner]])
        where = jnp.concatenate([slots[here][None], block_lists[step, here]])
        payload = pack(where, keys, values)
        arrived = exchange(masks[step], payload)
        keys, values = unpack(where, arrived, keys, values)
    valid = jnp.clip(counts[here] - place * SEG, 0, SEG)
    peers = jnp.stack([peer_at(place, offset) for offset in range(WIDTH)] + [place * OWN_NEW])
    peers = peers.astype(jnp.int32)
    pad = ((0, 0), (0, PAD_NEW - OWN_NEW), (0, 0))
    plan = jnp.arange(SLOTS, dtype=jnp.int32)
    partial, stats = attend(
        plan,
        valid[plan],
        peers,
        queries,
        keys,
        values,
        jnp.pad(new_keys[0], pad),
        jnp.pad(new_values[0], pad),
    )
    attended = combine(partial, stats)
    return (attended[None], keys[None], values[None])


def solution(mesh):
    placed = (
        P("group", None, None, "ctx"),
        P("group", None, "ctx", None),
        P("group", None, "ctx", None),
        P("group", None, "ctx", None),
        P("group", None, "ctx", None),
        P(),
        P(),
        P(),
        P(),
    )
    return jax.shard_map(
        shards,
        mesh=mesh,
        in_specs=placed,
        out_specs=(
            P("group", None, None, "ctx"),
            P("group", None, "ctx", None),
            P("group", None, "ctx", None),
        ),
        check_vma=False,
    )
```

```python
import functools
import math

import jax
import jax.numpy as jnp
from jax import lax
from jax.experimental import pallas as pl
from jax.experimental.pallas import tpu as pltpu
from jax.sharding import PartitionSpec as P

HD = 128
NEW = 32
MATCHINGS = 3
BLOCK = 128
GROUPS = 16
WIDTH = 8
SLOTS = 4
SEG = 512
NB = 4
FEATURES = 1024
GQ = 8
ROWS = GQ * NEW
OWN_NEW = 4
PAD_NEW = 16
MESH = pl.DeviceIdType.MESH
ANY = pl.ANY
BF16 = jnp.bfloat16
FACTOR = math.log2(math.e) / math.sqrt(HD)
LOWEST = -1e30
FLOOR = -1e29

WHERE = 0
ORDER = 24
VALID = 28
PEERS = 32
FIRST = 40
AGAIN = 41


def peer_at(place, offset):
    x, z = place // 2, place % 2
    return ((x + offset // 2) % 4) * 2 + (z + offset % 2) % 2


def estimate(bytes_accessed, flops=0):
    return pl.CostEstimate(flops=flops, bytes_accessed=bytes_accessed, transcendentals=0)


def plan_body(masks, movers, lists, lengths, table):
    here = lax.axis_index("group")
    place = lax.axis_index("ctx")
    for m in range(MATCHINGS):
        table[WHERE + 8 * m] = movers[m, here]
        for j in range(NB):
            table[WHERE + 8 * m + 1 + j] = lists[m, here, j]
    second, third = movers[1, here], movers[2, here]

    def rank(s):
        return jnp.where(third == s, 2, jnp.where(second == s, 1, 0))

    for s in range(SLOTS):
        spot = jnp.int32(0)
        for other in range(SLOTS):
            if other != s:
                ahead = rank(other) <= rank(s) if other < s else rank(other) < rank(s)
                spot += ahead.astype(jnp.int32)
        group, slot = here, jnp.int32(s)
        for m in reversed(range(MATCHINGS)):
            moved = movers[m, group] == slot
            group = jnp.where(moved, group ^ masks[m], group)
            slot = jnp.where(moved, movers[m, group], slot)
        table[ORDER + spot] = jnp.int32(s)
        table[VALID + spot] = jnp.clip(lengths[group, slot] - place * SEG, 0, SEG)
    for offset in range(WIDTH):
        table[PEERS + offset] = peer_at(place, offset)
    table[FIRST] = place * OWN_NEW
    for m in range(1, MATCHINGS):
        base = AGAIN + 5 * (m - 1)
        table[base] = (movers[m, here] == movers[m - 1, here]).astype(jnp.int32)
        for j in range(NB):
            spot = jnp.int32(0)
            for i in range(1, NB):
                spot = jnp.where(lists[m - 1, here, i] == lists[m, here, j], i, spot)
            table[base + 1 + j] = spot


def plan(masks, movers, lists, lengths):
    smem = pl.BlockSpec(memory_space=pltpu.SMEM)
    return pl.pallas_call(
        plan_body,
        in_specs=[smem] * 4,
        out_specs=smem,
        out_shape=jax.ShapeDtypeStruct((64,), jnp.int32),
        name="plan",
    )(masks, movers, lists, lengths)


def listed(matching):
    base = WHERE + 8 * matching
    return pl.BlockSpec((1, BLOCK, FEATURES), lambda j, t: (t[base], t[base + 1 + j], 0))


def packed():
    return pl.BlockSpec((2, 1, BLOCK, FEATURES), lambda j, t: (0, j, 0, 0))


def pack_body(table, keys_ref, values_ref, out_ref):
    out_ref[0, 0] = keys_ref[0]
    out_ref[1, 0] = values_ref[0]


def pack(matching, table, keys, values):
    return pl.pallas_call(
        pack_body,
        grid_spec=pltpu.PrefetchScalarGridSpec(
            num_scalar_prefetch=1,
            grid=(NB,),
            in_specs=[listed(matching)] * 2,
            out_specs=packed(),
        ),
        out_shape=jax.ShapeDtypeStruct((2, NB, BLOCK, FEATURES), BF16),
        cost_estimate=estimate(4 << 20),
        name="pack",
    )(table, keys, values)


def unpack_body(table, arrived_ref, keys_in, values_in, keys_ref, values_ref):
    keys_ref[0] = arrived_ref[0, 0]
    values_ref[0] = arrived_ref[1, 0]


def unpack(matching, table, arrived, keys, values):
    shape = jax.ShapeDtypeStruct(keys.shape, keys.dtype)
    return pl.pallas_call(
        unpack_body,
        grid_spec=pltpu.PrefetchScalarGridSpec(
            num_scalar_prefetch=1,
            grid=(NB,),
            in_specs=[packed()] + [pl.BlockSpec(memory_space=ANY)] * 2,
            out_specs=[listed(matching)] * 2,
        ),
        out_shape=[shape, shape],
        input_output_aliases={2: 0, 3: 1},
        cost_estimate=estimate(4 << 20),
        name="unpack",
    )(table, arrived, keys, values)


def again_body(matching, table, arrived, ready, out, held, into, outof):
    base = AGAIN + 5 * (matching - 1)

    @pl.when(table[base] == 1)
    def _():
        ins, outs = [], []
        for j in range(NB):
            ins.append(
                pltpu.make_async_copy(
                    arrived.at[:, pl.ds(table[base + 1 + j], 1)], held.at[j], into.at[j]
                )
            )
            outs.append(
                pltpu.make_async_copy(held.at[j], out.at[:, pl.ds(j, 1)], outof.at[j])
            )
        for copy in ins:
            copy.start()
        for j in range(NB):
            ins[j].wait()
            outs[j].start()
        for copy in outs:
            copy.wait()


def again(matching, table, arrived, ready):
    anywhere = pl.BlockSpec(memory_space=ANY)
    return pl.pallas_call(
        functools.partial(again_body, matching),
        grid_spec=pltpu.PrefetchScalarGridSpec(
            num_scalar_prefetch=1,
            grid=(),
            in_specs=[anywhere] * 2,
            out_specs=anywhere,
            scratch_shapes=[
                pltpu.VMEM((NB, 2, 1, BLOCK, FEATURES), BF16),
                pltpu.SemaphoreType.DMA((NB,)),
                pltpu.SemaphoreType.DMA((NB,)),
            ],
        ),
        out_shape=jax.ShapeDtypeStruct(ready.shape, ready.dtype),
        input_output_aliases={2: 0},
        cost_estimate=estimate(4 << 20),
        name="again",
    )(table, arrived, ready)


def duplicate_body(keys_in, values_in, keys_ref, values_ref):
    keys_ref[...] = keys_in[...]
    values_ref[...] = values_in[...]


def duplicate(keys, values):
    spec = pl.BlockSpec((1, SEG // 2, FEATURES), lambda i: (i // 2, i % 2, 0))
    shape = jax.ShapeDtypeStruct(keys.shape, keys.dtype)
    return pl.pallas_call(
        duplicate_body,
        grid=(2 * SLOTS,),
        in_specs=[spec] * 2,
        out_specs=[spec] * 2,
        out_shape=[shape] * 2,
        cost_estimate=estimate(16 << 20),
        name="duplicate",
    )(keys, values)


def gather_body(q_ref, out_ref, send, arrive, local):
    group = lax.axis_index("group")
    place = lax.axis_index("ctx")
    x, z = place // 2, place % 2
    across = x * 2 + (z + 1) % 2
    behind = [((x + 4 - dx) % 4) * 2 + z for dx in range(4)]
    barrier = pltpu.get_barrier_semaphore()
    for peer in behind[1:] + [across]:
        pl.semaphore_signal(barrier, inc=1, device_id=(group, peer), device_id_type=MESH)
    own = pltpu.make_async_copy(q_ref, out_ref.at[0], local)
    own.start()
    pl.semaphore_wait(barrier, 4)

    def push(src, slot, peer):
        copy = pltpu.make_async_remote_copy(
            src_ref=src,
            dst_ref=out_ref.at[slot],
            send_sem=send.at[slot],
            recv_sem=arrive.at[slot],
            device_id=(group, peer),
            device_id_type=MESH,
        )
        copy.start()
        return copy

    first = push(q_ref, 1, across)
    rest = [push(q_ref, 2 * dx, behind[dx]) for dx in (1, 3, 2)]
    first.wait_recv()
    rest += [push(out_ref.at[1], 2 * dx + 1, behind[dx]) for dx in (1, 3, 2)]
    first.wait_send()
    own.wait()
    for copy in rest:
        copy.wait()


def gather(query):
    anywhere = pl.BlockSpec(memory_space=ANY)
    dma = pltpu.SemaphoreType.DMA((WIDTH,))
    return pl.pallas_call(
        gather_body,
        in_specs=[anywhere],
        out_specs=anywhere,
        out_shape=jax.ShapeDtypeStruct((WIDTH,) + query.shape, query.dtype),
        scratch_shapes=[dma, dma, pltpu.SemaphoreType.DMA],
        compiler_params=pltpu.CompilerParams(collective_id=0, has_side_effects=True),
        cost_estimate=estimate(60 << 20),
        name="gather",
    )(query)


def attend_body(at, table, q_ref, k_ref, v_ref, nk_ref, nv_ref, o_ref, s_ref):
    count = table[VALID + at + pl.program_id(0)]
    q = q_ref[0, 0]
    rows = jnp.concatenate([q[:, g * HD : (g + 1) * HD] for g in range(GQ)], axis=0)
    contract_last = (((1,), (1,)), ((), ()))
    contract_first = (((0,), (0,)), ((), ()))
    older = lax.dot_general(k_ref[0], rows, contract_last, preferred_element_type=jnp.float32)
    newer = lax.dot_general(nk_ref[0], rows, contract_last, preferred_element_type=jnp.float32)
    position = lax.broadcasted_iota(jnp.int32, older.shape, 0)
    fresh = lax.broadcasted_iota(jnp.int32, newer.shape, 0)
    token = lax.broadcasted_iota(jnp.int32, newer.shape, 1) % NEW
    valid_new = jnp.logical_and(fresh < OWN_NEW, table[FIRST] + fresh <= token)
    older = jnp.where(position < count, older, LOWEST)
    newer = jnp.where(valid_new, newer, LOWEST)
    top = jnp.maximum(
        jnp.max(older, axis=0, keepdims=True), jnp.max(newer, axis=0, keepdims=True)
    )
    top = jnp.maximum(top, FLOOR)
    exp_old = jnp.exp2((older - top) * FACTOR)
    exp_new = jnp.exp2((newer - top) * FACTOR)
    total = jnp.sum(exp_old, axis=0, keepdims=True) + jnp.sum(exp_new, axis=0, keepdims=True)
    summed = lax.dot_general(
        v_ref[0], exp_old.astype(BF16), contract_first, preferred_element_type=jnp.float32
    )
    summed += lax.dot_general(
        nv_ref[0], exp_new.astype(BF16), contract_first, preferred_element_type=jnp.float32
    )
    o_ref[0, 0] = summed.astype(BF16)
    row = lax.broadcasted_iota(jnp.int32, (8, ROWS), 0)
    s_ref[0, 0] = jnp.where(row == 0, top, total)


def attend(at, n, table, queries, keys, values, new_keys, new_values):
    def column(rows):
        return pl.BlockSpec((1, rows, HD), lambda i, o, t: (t[ORDER + at + i], 0, t[PEERS + o]))

    def owned(rows):
        return pl.BlockSpec((1, 1, rows, ROWS), lambda i, o, t: (t[PEERS + o], i, 0, 0))

    return pl.pallas_call(
        functools.partial(attend_body, at),
        grid_spec=pltpu.PrefetchScalarGridSpec(
            num_scalar_prefetch=1,
            grid=(n, WIDTH),
            in_specs=[
                pl.BlockSpec(
                    (1, 1, NEW, GQ * HD), lambda i, o, t: (o, t[ORDER + at + i], 0, 0)
                ),
                column(SEG),
                column(SEG),
                column(PAD_NEW),
                column(PAD_NEW),
            ],
            out_specs=[owned(HD), owned(8)],
        ),
        out_shape=[
            jax.ShapeDtypeStruct((WIDTH, n, HD, ROWS), BF16),
            jax.ShapeDtypeStruct((WIDTH, n, 8, ROWS), jnp.float32),
        ],
        cost_estimate=estimate(n * (24 << 20)),
        name="attend",
    )(table, queries, keys, values, new_keys, new_values)


def combine_body(n, o_ref, s_ref, out_ref, o_all, s_all, sem_o, sem_s, arrive_o, arrive_s, local):
    group = lax.axis_index("group")
    place = lax.axis_index("ctx")
    barrier = pltpu.get_barrier_semaphore()
    for offset in range(1, WIDTH):
        pl.semaphore_signal(
            barrier, inc=1, device_id=(group, peer_at(place, offset)), device_id_type=MESH
        )
    own_o = pltpu.make_async_copy(o_ref.at[place], o_all.at[0], local.at[0])
    own_s = pltpu.make_async_copy(s_ref.at[place], s_all.at[0], local.at[1])
    own_o.start()
    own_s.start()
    pl.semaphore_wait(barrier, WIDTH - 1)
    sends = []
    for offset in (4, 5, 2, 6, 3, 7, 1):
        peer = peer_at(place, offset)
        for src, dst, send, recv in (
            (o_ref, o_all, sem_o, arrive_o),
            (s_ref, s_all, sem_s, arrive_s),
        ):
            copy = pltpu.make_async_remote_copy(
                src_ref=src.at[peer],
                dst_ref=dst.at[offset],
                send_sem=send.at[offset],
                recv_sem=recv.at[offset],
                device_id=(group, peer),
                device_id_type=MESH,
            )
            copy.start()
            sends.append(copy)
    own_o.wait()
    own_s.wait()
    for copy in sends:
        copy.wait()
    def merge(i, _):
        def tops(offset, top):
            return jnp.maximum(top, s_all[offset, i, 0:1])

        top = lax.fori_loop(1, WIDTH, tops, s_all[0, i, 0:1])

        def add(offset, sums):
            total, merged = sums
            scale = jnp.exp2((s_all[offset, i, 0:1] - top) * FACTOR)
            total += scale * s_all[offset, i, 1:2]
            return total, merged + o_all[offset, i].astype(jnp.float32) * scale

        total, merged = lax.fori_loop(
            0, WIDTH, add, (jnp.zeros((1, ROWS), jnp.float32), jnp.zeros((HD, ROWS), jnp.float32))
        )
        rows = jnp.transpose(merged / total)
        for g in range(GQ):
            out_ref[i, :, g * HD : (g + 1) * HD] = rows[g * NEW : (g + 1) * NEW].astype(BF16)
        return 0

    lax.fori_loop(0, n, merge, 0)


def combine(partial, stats):
    n = partial.shape[1]
    dma = pltpu.SemaphoreType.DMA((WIDTH,))
    return pl.pallas_call(
        functools.partial(combine_body, n),
        in_specs=[pl.BlockSpec(memory_space=ANY)] * 2,
        out_specs=pl.BlockSpec(memory_space=pltpu.VMEM),
        out_shape=jax.ShapeDtypeStruct((n, NEW, GQ * HD), BF16),
        scratch_shapes=[
            pltpu.VMEM((WIDTH, n, HD, ROWS), BF16),
            pltpu.VMEM((WIDTH, n, 8, ROWS), jnp.float32),
            dma,
            dma,
            dma,
            dma,
            pltpu.SemaphoreType.DMA((2,)),
        ],
        compiler_params=pltpu.CompilerParams(collective_id=n, has_side_effects=True),
        cost_estimate=estimate(n * (24 << 20)),
        name="combine",
    )(partial, stats)


def settle_body(table, *refs):
    out_ref = refs[-1]
    at = 0
    for ref in refs[:-1]:
        for i in range(ref.shape[0]):
            out_ref[table[ORDER + at]] = ref[i]
            at += 1


def settle(table, *parts):
    shape = (SLOTS, NEW, GQ * HD)

    def whole(shape):
        return pl.BlockSpec(shape, lambda i, t: (0, 0, 0))

    return pl.pallas_call(
        settle_body,
        grid_spec=pltpu.PrefetchScalarGridSpec(
            num_scalar_prefetch=1,
            grid=(1,),
            in_specs=[whole(part.shape) for part in parts],
            out_specs=whole(shape),
        ),
        out_shape=jax.ShapeDtypeStruct(shape, BF16),
        cost_estimate=estimate(1 << 20),
        name="settle",
    )(table, *parts)


def matched(mask, run, *args):
    def branch(d):
        route = [(g, g ^ d) for g in range(GROUPS)]
        return functools.partial(run, lambda block: lax.ppermute(block, "group", route))

    return lax.switch(mask - 1, [branch(d) for d in range(1, GROUPS)], *args)


def shards(
    query, cache_keys, cache_values, new_keys, new_values, masks, movers, block_lists, lengths
):
    table = plan(masks, movers, block_lists, lengths)
    pad = ((0, 0), (0, PAD_NEW - OWN_NEW), (0, 0))
    new_keys = jnp.pad(new_keys[0], pad)
    new_values = jnp.pad(new_values[0], pad)

    def first(permute, table, payload, query, keys, values):
        arrived = permute(payload)
        queries = gather(query)
        ready = pack(1, table, keys, values)
        keys, values = duplicate(keys, values)
        return arrived, queries, ready, keys, values

    def second(permute, table, payload, arrived, queries, keys, values, new_keys, new_values):
        now = permute(payload)
        keys, values = unpack(0, table, arrived, keys, values)
        ready = pack(2, table, keys, values)
        partial = attend(0, 2, table, queries, keys, values, new_keys, new_values)
        return now, ready, combine(*partial), keys, values

    def third(permute, table, payload, arrived, queries, keys, values, new_keys, new_values):
        now = permute(payload)
        keys, values = unpack(1, table, arrived, keys, values)
        partial = attend(2, 1, table, queries, keys, values, new_keys, new_values)
        return now, combine(*partial), keys, values

    payload = pack(0, table, cache_keys[0], cache_values[0])
    arrived, queries, ready, keys, values = matched(
        masks[0], first, table, payload, query[0], cache_keys[0], cache_values[0]
    )
    payload = again(1, table, arrived, ready)
    arrived, ready, early, keys, values = matched(
        masks[1], second, table, payload, arrived, queries, keys, values, new_keys, new_values
    )
    payload = again(2, table, arrived, ready)
    arrived, late, keys, values = matched(
        masks[2], third, table, payload, arrived, queries, keys, values, new_keys, new_values
    )
    keys, values = unpack(2, table, arrived, keys, values)
    last = combine(*attend(3, 1, table, queries, keys, values, new_keys, new_values))
    attended = settle(table, early, late, last)
    return (attended[None], keys[None], values[None])


def solution(mesh):
    placed = (
        P("group", None, None, "ctx"),
        P("group", None, "ctx", None),
        P("group", None, "ctx", None),
        P("group", None, "ctx", None),
        P("group", None, "ctx", None),
        P(),
        P(),
        P(),
        P(),
    )
    return jax.shard_map(
        shards,
        mesh=mesh,
        in_specs=placed,
        out_specs=(
            P("group", None, None, "ctx"),
            P("group", None, "ctx", None),
            P("group", None, "ctx", None),
        ),
        check_vma=False,
    )
```

```python
import functools
import math

import jax
import jax.numpy as jnp
from jax import lax
from jax.experimental import pallas as pl
from jax.experimental.pallas import tpu as pltpu
from jax.sharding import PartitionSpec as P

HD = 128
NEW = 32
MATCHINGS = 3
BLOCK = 128
GROUPS = 16
WIDTH = 8
SLOTS = 4
SEG = 512
NB = 4
FEATURES = 1024
GQ = 8
ROWS = GQ * NEW
OWN_NEW = 4
PAD_NEW = 16
MESH = pl.DeviceIdType.MESH
ANY = pl.ANY
BF16 = jnp.bfloat16
FACTOR = math.log2(math.e) / math.sqrt(HD)
LOWEST = -1e30
FLOOR = -1e29

WHERE = 0
ORDER = 24
VALID = 28
PEERS = 32
FIRST = 40
AGAIN = 41
PAIRS = 52


def peer_at(place, offset):
    x, z = place // 2, place % 2
    return ((x + offset // 2) % 4) * 2 + (z + offset % 2) % 2


def estimate(bytes_accessed, flops=0):
    return pl.CostEstimate(flops=flops, bytes_accessed=bytes_accessed, transcendentals=0)


def plan_body(masks, movers, lists, lengths, table, *branches):
    here = lax.axis_index("group")
    place = lax.axis_index("ctx")
    for m in range(MATCHINGS):
        branches[m][0] = masks[m] - 1
        table[WHERE + 8 * m] = movers[m, here]
        for j in range(NB):
            table[WHERE + 8 * m + 1 + j] = lists[m, j, here]
    second, third = movers[1, here], movers[2, here]

    def rank(s):
        return jnp.where(third == s, 2, jnp.where(second == s, 1, 0))

    for s in range(SLOTS):
        spot = jnp.int32(0)
        for other in range(SLOTS):
            if other != s:
                ahead = rank(other) <= rank(s) if other < s else rank(other) < rank(s)
                spot += ahead.astype(jnp.int32)
        group, slot = here, jnp.int32(s)
        for m in reversed(range(MATCHINGS)):
            moved = movers[m, group] == slot
            group = jnp.where(moved, group ^ masks[m], group)
            slot = jnp.where(moved, movers[m, group], slot)
        table[ORDER + spot] = jnp.int32(s)
        table[VALID + spot] = jnp.clip(lengths[slot, group] - place * SEG, 0, SEG)
    for offset in range(WIDTH):
        table[PEERS + offset] = peer_at(place, offset)
    table[FIRST] = place * OWN_NEW
    for dx in range(WIDTH // 2):
        table[PAIRS + dx] = peer_at(place, 2 * dx) // 2
    for m in range(1, MATCHINGS):
        base = AGAIN + 5 * (m - 1)
        table[base] = (movers[m, here] == movers[m - 1, here]).astype(jnp.int32)
        for j in range(NB):
            spot = jnp.int32(0)
            for i in range(1, NB):
                spot = jnp.where(lists[m - 1, i, here] == lists[m, j, here], i, spot)
            table[base + 1 + j] = spot


def plan(masks, movers, lists, lengths):
    smem = pl.BlockSpec(memory_space=pltpu.SMEM)
    return pl.pallas_call(
        plan_body,
        in_specs=[smem] * 4,
        out_specs=[smem] * 4,
        out_shape=[jax.ShapeDtypeStruct((64,), jnp.int32)]
        + [jax.ShapeDtypeStruct((1,), jnp.int32)] * MATCHINGS,
        name="plan",
    )(masks, movers, jnp.transpose(lists, (0, 2, 1)), jnp.transpose(lengths))


ANYWHERE = pl.BlockSpec(memory_space=ANY)
CACHE = jax.ShapeDtypeStruct((SLOTS, SEG, FEATURES), BF16)
PAYLOAD = jax.ShapeDtypeStruct((2, NB, BLOCK, FEATURES), BF16)
HELD = pltpu.VMEM((NB, 2, BLOCK, FEATURES), BF16)


def in_order(body, start=0, stop=NB):
    def step(j, carry):
        body(j)
        return carry

    lax.fori_loop(start, stop, step, 0)


def copied(src, dst, sem):
    return pltpu.make_async_copy(src, dst, sem)


def block_of(ref, table, matching, j):
    base = WHERE + 8 * matching
    row = pl.multiple_of(table[base + 1 + j] * BLOCK, BLOCK)
    return ref.at[table[base], pl.ds(row, BLOCK)]


def take(matching, table, keys, values, out, held, into, outof):
    def fetch(j, half):
        ref = (keys, values)[half]
        return copied(block_of(ref, table, matching, j), held.at[j, half], into.at[j, half])

    def store(j):
        return copied(held.at[j], out.at[:, j], outof.at[j, 0])

    def start(j):
        fetch(j, 0).start()
        fetch(j, 1).start()

    def turn(j):
        fetch(j, 0).wait()
        fetch(j, 1).wait()
        store(j).start()

    in_order(start)
    in_order(turn)
    in_order(lambda j: store(j).wait())


def put(matching, table, arrived, keys, values, held, into, outof):
    def fetch(j):
        return copied(arrived.at[:, j], held.at[j], into.at[j, 0])

    def store(j, half):
        ref = (keys, values)[half]
        return copied(held.at[j, half], block_of(ref, table, matching, j), outof.at[j, half])

    def turn(j):
        fetch(j).wait()
        store(j, 0).start()
        store(j, 1).start()

    def finish(j):
        store(j, 0).wait()
        store(j, 1).wait()

    in_order(lambda j: fetch(j).start())
    in_order(turn)
    in_order(finish)


def blocks(body, name, n_out, aliases, *args):
    shapes = [CACHE, CACHE] * (n_out // 2) + [PAYLOAD] * (n_out % 2)
    sem = pltpu.SemaphoreType.DMA((NB, 2))
    return pl.pallas_call(
        body,
        grid_spec=pltpu.PrefetchScalarGridSpec(
            num_scalar_prefetch=1,
            grid=(),
            in_specs=[ANYWHERE] * (len(args) - 1),
            out_specs=[ANYWHERE] * n_out,
            scratch_shapes=[HELD, sem, sem],
        ),
        out_shape=shapes,
        input_output_aliases=aliases,
        cost_estimate=estimate(8 << 20),
        name=name,
    )(*args)


def pack(table, keys, values):
    def body(table, keys, values, out, held, into, outof):
        take(0, table, keys, values, out, held, into, outof)

    return blocks(body, "pack", 1, {}, table, keys, values)[0]


def unpack(matching, table, arrived, keys, values):
    def body(table, arrived, keys_in, values_in, keys, values, held, into, outof):
        put(matching, table, arrived, keys, values, held, into, outof)

    return blocks(body, "unpack", 2, {2: 0, 3: 1}, table, arrived, keys, values)


def renew(table, arrived, keys, values):
    def body(table, arrived, keys_in, values_in, keys, values, out, held, into, outof):
        put(0, table, arrived, keys, values, held, into, outof)
        take(2, table, keys, values, out, held, into, outof)

    return blocks(body, "renew", 3, {2: 0, 3: 1}, table, arrived, keys, values)


def again(matching, table, arrived, ready):
    base = AGAIN + 5 * (matching - 1)

    def body(table, arrived, ready, out, held, into, outof):
        def fetch(j):
            return copied(arrived.at[:, table[base + 1 + j]], held.at[j], into.at[j, 0])

        def store(j):
            return copied(held.at[j], out.at[:, j], outof.at[j, 0])

        def turn(j):
            fetch(j).wait()
            store(j).start()

        @pl.when(table[base] == 1)
        def _():
            in_order(lambda j: fetch(j).start())
            in_order(turn)
            in_order(lambda j: store(j).wait())

    return blocks(body, "again", 1, {2: 0}, table, arrived, ready)[0]


def stage_body(table, keys_in, values_in, keys, values, out, k_held, v_held, sem, back, pick):
    def fetch(i, half):
        src, dst = ((keys_in, k_held), (values_in, v_held))[half]
        return copied(src.at[i], dst.at[i], sem.at[i, half])

    def store(i, half):
        src, dst = ((k_held, keys), (v_held, values))[half]
        return copied(src.at[i], dst.at[i], back.at[i, half])

    def select(j, half):
        src = (k_held, v_held)[half]
        return copied(block_of(src, table, 1, j), out.at[half, j], pick.at[j, half])

    def start(i):
        fetch(i, 0).start()
        fetch(i, 1).start()

    def turn(i):
        fetch(i, 0).wait()
        store(i, 0).start()
        fetch(i, 1).wait()
        store(i, 1).start()

    def choose(j):
        select(j, 0).start()
        select(j, 1).start()

    def finish(j):
        select(j, 0).wait()
        select(j, 1).wait()
        store(j, 0).wait()
        store(j, 1).wait()

    in_order(start)
    in_order(turn)
    in_order(choose)
    in_order(finish)


def stage(table, keys, values):
    sem = pltpu.SemaphoreType.DMA((NB, 2))
    held = pltpu.VMEM(CACHE.shape, BF16)
    return pl.pallas_call(
        stage_body,
        grid_spec=pltpu.PrefetchScalarGridSpec(
            num_scalar_prefetch=1,
            grid=(),
            in_specs=[ANYWHERE] * 2,
            out_specs=[ANYWHERE] * 3,
            scratch_shapes=[held, held, sem, sem, sem],
        ),
        out_shape=[CACHE, CACHE, PAYLOAD],
        cost_estimate=estimate(20 << 20),
        name="stage",
    )(table, keys, values)


def gather_body(q_ref, across_ref, out_ref, send, arrive, local):
    group = lax.axis_index("group")
    place = lax.axis_index("ctx")
    x, z = place // 2, place % 2

    def behind(dx):
        return ((x + 4 - dx) % 4) * 2 + z

    barrier = pltpu.get_barrier_semaphore()
    in_order(
        lambda dx: pl.semaphore_signal(
            barrier, inc=1, device_id=(group, behind(dx)), device_id_type=MESH
        ),
        1,
    )
    own = [
        copied(src, out_ref.at[half], local.at[half])
        for half, src in enumerate((q_ref, across_ref))
    ]
    for copy in own:
        copy.start()
    pl.semaphore_wait(barrier, 3)

    def push(dx, half):
        slot = 2 * dx + half
        return pltpu.make_async_remote_copy(
            src_ref=(q_ref, across_ref)[half],
            dst_ref=out_ref.at[slot],
            send_sem=send.at[slot],
            recv_sem=arrive.at[slot],
            device_id=(group, behind(dx)),
            device_id_type=MESH,
        )

    def start(dx):
        push(dx, 0).start()
        push(dx, 1).start()

    def finish(dx):
        push(dx, 0).wait()
        push(dx, 1).wait()

    in_order(start, 1)
    for copy in own:
        copy.wait()
    in_order(finish, 1)


def gather(query, across):
    dma = pltpu.SemaphoreType.DMA((WIDTH,))
    return pl.pallas_call(
        gather_body,
        in_specs=[ANYWHERE] * 2,
        out_specs=ANYWHERE,
        out_shape=jax.ShapeDtypeStruct((WIDTH,) + query.shape, query.dtype),
        scratch_shapes=[dma, dma, pltpu.SemaphoreType.DMA((2,))],
        compiler_params=pltpu.CompilerParams(collective_id=0, has_side_effects=True),
        cost_estimate=estimate(60 << 20),
        name="gather",
    )(query, across)


CONTRACT_LAST = (((1,), (1,)), ((), ()))
CONTRACT_FIRST = (((0,), (0,)), ((), ()))


def rows_of(q):
    return jnp.concatenate([q[:, g * HD : (g + 1) * HD] for g in range(GQ)], axis=0)


def times(a, b, contract):
    return lax.dot_general(a, b, contract, preferred_element_type=jnp.float32)


def fresh_scores(new_keys, rows, first):
    scores = times(new_keys, rows, CONTRACT_LAST)
    fresh = lax.broadcasted_iota(jnp.int32, scores.shape, 0)
    token = lax.broadcasted_iota(jnp.int32, scores.shape, 1) % NEW
    seen = jnp.logical_and(fresh < OWN_NEW, first + fresh <= token)
    return jnp.where(seen, scores, LOWEST)


def stats_of(top, total):
    row = lax.broadcasted_iota(jnp.int32, (8, ROWS), 0)
    return jnp.where(row == 0, top, total)


def attend_body(at, table, q_ref, k_ref, v_ref, nk_ref, nv_ref, o_ref, s_ref, held):
    count = table[VALID + at + pl.program_id(0)]
    rows = rows_of(q_ref[0, 0])
    newer = fresh_scores(nk_ref[0], rows, table[FIRST])
    within = lax.broadcasted_iota(jnp.int32, (BLOCK, ROWS), 0)

    def chunk(c):
        return pl.ds(pl.multiple_of(c * BLOCK, BLOCK), BLOCK)

    def score(c, top):
        scores = times(k_ref[0, chunk(c)], rows, CONTRACT_LAST)
        scores = jnp.where(within < count - c * BLOCK, scores, LOWEST)
        held[chunk(c)] = scores
        return jnp.maximum(top, jnp.max(scores, axis=0, keepdims=True))

    top = jnp.maximum(jnp.max(newer, axis=0, keepdims=True), FLOOR)
    top = lax.fori_loop(0, NB, score, top)
    exp_new = jnp.exp2((newer - top) * FACTOR)

    def weigh(c, sums):
        total, summed = sums
        weights = jnp.exp2((held[chunk(c)] - top) * FACTOR)
        total += jnp.sum(weights, axis=0, keepdims=True)
        return total, summed + times(v_ref[0, chunk(c)], weights.astype(BF16), CONTRACT_FIRST)

    total = jnp.sum(exp_new, axis=0, keepdims=True)
    summed = times(nv_ref[0], exp_new.astype(BF16), CONTRACT_FIRST)
    total, summed = lax.fori_loop(0, NB, weigh, (total, summed))
    o_ref[0, 0] = summed.astype(BF16)
    s_ref[0, 0] = stats_of(top, total)


def partials(n):
    return [
        jax.ShapeDtypeStruct((WIDTH, n, HD, ROWS), BF16),
        jax.ShapeDtypeStruct((WIDTH, n, 8, ROWS), jnp.float32),
    ]


def attend(at, n, table, queries, keys, values, new_keys, new_values):
    def column(rows):
        return pl.BlockSpec((1, rows, HD), lambda i, o, t: (t[ORDER + at + i], 0, t[PEERS + o]))

    def owned(rows):
        return pl.BlockSpec((1, 1, rows, ROWS), lambda i, o, t: (t[PEERS + o], i, 0, 0))

    return pl.pallas_call(
        functools.partial(attend_body, at),
        grid_spec=pltpu.PrefetchScalarGridSpec(
            num_scalar_prefetch=1,
            grid=(n, WIDTH),
            in_specs=[
                pl.BlockSpec(
                    (1, 1, NEW, GQ * HD), lambda i, o, t: (o, t[ORDER + at + i], 0, 0)
                ),
                column(SEG),
                column(SEG),
                column(PAD_NEW),
                column(PAD_NEW),
            ],
            out_specs=[owned(HD), owned(8)],
            scratch_shapes=[pltpu.VMEM((SEG, ROWS), jnp.float32)],
        ),
        out_shape=partials(n),
        cost_estimate=estimate(n * (24 << 20)),
        name="attend",
    )(table, queries, keys, values, new_keys, new_values)


def finish_body(
    table, q_ref, arrived, nk_ref, nv_ref, keys_in, values_in, o_ref, s_ref, keys, values, outof
):
    def store(j, half):
        ref = (keys, values)[half]
        return copied(arrived.at[half, j], block_of(ref, table, 2, j), outof.at[j, half])

    for j in range(NB):
        store(j, 0).start()
        store(j, 1).start()
    slot = table[ORDER + SLOTS - 1]
    count = table[VALID + SLOTS - 1]
    within = lax.broadcasted_iota(jnp.int32, (BLOCK, ROWS), 0)
    starts = [table[WHERE + 16 + 1 + j] * BLOCK for j in range(NB)]

    def pair(dx):
        for offset in range(2):
            head = table[PEERS + 2 * dx + offset]
            lanes = pl.ds(pl.multiple_of(head * HD, HD), HD)
            rows = rows_of(q_ref[2 * dx + offset, slot])
            newer = fresh_scores(nk_ref[slot, :, lanes], rows, table[FIRST])
            older = times(
                arrived[0, :, :, lanes].reshape(SEG, HD), rows, CONTRACT_LAST
            )
            older = jnp.concatenate(
                [
                    jnp.where(
                        within < count - starts[j], older[j * BLOCK : (j + 1) * BLOCK], LOWEST
                    )
                    for j in range(NB)
                ]
            )
            top = jnp.maximum(
                jnp.max(older, axis=0, keepdims=True), jnp.max(newer, axis=0, keepdims=True)
            )
            top = jnp.maximum(top, FLOOR)
            old = jnp.exp2((older - top) * FACTOR)
            new = jnp.exp2((newer - top) * FACTOR)
            total = jnp.sum(old, axis=0, keepdims=True) + jnp.sum(new, axis=0, keepdims=True)
            summed = times(
                arrived[1, :, :, lanes].reshape(SEG, HD), old.astype(BF16), CONTRACT_FIRST
            )
            summed += times(nv_ref[slot, :, lanes], new.astype(BF16), CONTRACT_FIRST)
            o_ref[head, 0] = summed.astype(BF16)
            s_ref[head, 0] = stats_of(top, total)

    in_order(pair, 0, WIDTH // 2)
    for j in range(NB):
        store(j, 0).wait()
        store(j, 1).wait()


def finish(table, queries, arrived, new_keys, new_values, keys, values):
    inside = pl.BlockSpec(memory_space=pltpu.VMEM)
    return pl.pallas_call(
        finish_body,
        grid_spec=pltpu.PrefetchScalarGridSpec(
            num_scalar_prefetch=1,
            grid=(),
            in_specs=[inside] * 4 + [ANYWHERE] * 2,
            out_specs=[inside] * 2 + [ANYWHERE] * 2,
            scratch_shapes=[pltpu.SemaphoreType.DMA((NB, 2))],
        ),
        out_shape=partials(1) + [CACHE, CACHE],
        input_output_aliases={5: 2, 6: 3},
        cost_estimate=estimate(24 << 20),
        name="finish",
    )(table, queries, arrived, new_keys, new_values, keys, values)


def fold(shares, read_top, read_total, read_sum):
    top = lax.fori_loop(1, shares, lambda j, t: jnp.maximum(t, read_top(j)), read_top(0))

    def add(j, sums):
        total, merged = sums
        scale = jnp.exp2((read_top(j) - top) * FACTOR)
        return total + scale * read_total(j), merged + read_sum(j) * scale

    zero = (jnp.zeros((1, ROWS), jnp.float32), jnp.zeros((HD, ROWS), jnp.float32))
    return (top,) + lax.fori_loop(0, shares, add, zero)


def write_rows(out_ref, i, merged, total):
    rows = jnp.transpose(merged / total)
    for g in range(GQ):
        out_ref[i, :, g * HD : (g + 1) * HD] = rows[g * NEW : (g + 1) * NEW].astype(BF16)


def reduce_body(
    n, o_ref, s_ref, out_ref, o_all, s_all, o_mid, s_mid, o_in, s_in, send, arrive, local
):
    group = lax.axis_index("group")
    place = lax.axis_index("ctx")
    x, z = place // 2, place % 2
    across = x * 2 + (z + 1) % 2

    def pair_at(dx):
        return pl.ds(2 * ((x + dx) % 4), 2)

    def push(dx, half):
        src, dst = ((o_ref, o_all), (s_ref, s_all))[half]
        return pltpu.make_async_remote_copy(
            src_ref=src.at[pair_at(dx)],
            dst_ref=dst.at[dx],
            send_sem=send.at[dx, half],
            recv_sem=arrive.at[dx, half],
            device_id=(group, ((x + dx) % 4) * 2 + z),
            device_id_type=MESH,
        )

    def swap(half):
        src, dst = ((o_mid, o_in), (s_mid, s_in))[half]
        return pltpu.make_async_remote_copy(
            src_ref=src.at[0],
            dst_ref=dst,
            send_sem=send.at[0, half],
            recv_sem=arrive.at[0, half],
            device_id=(group, across),
            device_id_type=MESH,
        )

    def own(half):
        src, dst = ((o_ref, o_all), (s_ref, s_all))[half]
        return copied(src.at[pair_at(0)], dst.at[0], local.at[half])

    def start(dx):
        push(dx, 0).start()
        push(dx, 1).start()

    def done(dx):
        push(dx, 0).wait()
        push(dx, 1).wait()

    barrier = pltpu.get_barrier_semaphore()
    in_order(
        lambda dx: pl.semaphore_signal(
            barrier, inc=1, device_id=(group, ((x + dx) % 4) * 2 + z), device_id_type=MESH
        ),
        1,
    )
    pl.semaphore_signal(barrier, inc=1, device_id=(group, across), device_id_type=MESH)
    own(0).start()
    own(1).start()
    pl.semaphore_wait(barrier, 4)
    in_order(start, 1)
    own(0).wait()
    own(1).wait()
    in_order(done, 1)

    def part(k):
        whose = (z + 1 + k) % 2

        def slot(i):
            top, total, merged = fold(
                4,
                lambda j: s_all[j, whose, i, 0:1],
                lambda j: s_all[j, whose, i, 1:2],
                lambda j: o_all[j, whose, i].astype(jnp.float32),
            )
            o_mid[k, i] = merged
            s_mid[k, i] = stats_of(top, total)

        in_order(slot, 0, n)

    in_order(part, 0, 2)
    swap(0).start()
    swap(1).start()
    swap(0).wait()
    swap(1).wait()

    def join(i):
        left, right = s_mid[1, i], s_in[i]
        top = jnp.maximum(left[0:1], right[0:1])
        a = jnp.exp2((left[0:1] - top) * FACTOR)
        b = jnp.exp2((right[0:1] - top) * FACTOR)
        total = a * left[1:2] + b * right[1:2]
        write_rows(out_ref, i, o_mid[1, i] * a + o_in[i] * b, total)

    in_order(join, 0, n)


def reduce(partial, stats):
    n = partial.shape[1]
    dma = pltpu.SemaphoreType.DMA((4, 2))
    return pl.pallas_call(
        functools.partial(reduce_body, n),
        in_specs=[ANYWHERE] * 2,
        out_specs=pl.BlockSpec(memory_space=pltpu.VMEM),
        out_shape=jax.ShapeDtypeStruct((n, NEW, GQ * HD), BF16),
        scratch_shapes=[
            pltpu.VMEM((4, 2, n, HD, ROWS), BF16),
            pltpu.VMEM((4, 2, n, 8, ROWS), jnp.float32),
            pltpu.VMEM((2, n, HD, ROWS), jnp.float32),
            pltpu.VMEM((2, n, 8, ROWS), jnp.float32),
            pltpu.VMEM((n, HD, ROWS), jnp.float32),
            pltpu.VMEM((n, 8, ROWS), jnp.float32),
            dma,
            dma,
            pltpu.SemaphoreType.DMA((2,)),
        ],
        compiler_params=pltpu.CompilerParams(collective_id=1 + n, has_side_effects=True),
        cost_estimate=estimate(n * (24 << 20)),
        name="reduce",
    )(partial, stats)


def combine_body(o_ref, s_ref, out_ref, o_all, s_all, sem_o, sem_s, arrive_o, arrive_s, local):
    group = lax.axis_index("group")
    place = lax.axis_index("ctx")
    barrier = pltpu.get_barrier_semaphore()
    for offset in range(1, WIDTH):
        pl.semaphore_signal(
            barrier, inc=1, device_id=(group, peer_at(place, offset)), device_id_type=MESH
        )
    own_o = pltpu.make_async_copy(o_ref.at[place], o_all.at[0], local.at[0])
    own_s = pltpu.make_async_copy(s_ref.at[place], s_all.at[0], local.at[1])
    own_o.start()
    own_s.start()
    pl.semaphore_wait(barrier, WIDTH - 1)
    sends = []
    for offset in (4, 5, 2, 6, 3, 7, 1):
        peer = peer_at(place, offset)
        for src, dst, send, recv in (
            (o_ref, o_all, sem_o, arrive_o),
            (s_ref, s_all, sem_s, arrive_s),
        ):
            copy = pltpu.make_async_remote_copy(
                src_ref=src.at[peer],
                dst_ref=dst.at[offset],
                send_sem=send.at[offset],
                recv_sem=recv.at[offset],
                device_id=(group, peer),
                device_id_type=MESH,
            )
            copy.start()
            sends.append(copy)
    own_o.wait()
    own_s.wait()
    for copy in sends:
        copy.wait()
    stats = [s_all[offset, 0] for offset in range(WIDTH)]
    top = functools.reduce(jnp.maximum, [part[0:1] for part in stats])
    scales = [jnp.exp2((part[0:1] - top) * FACTOR) for part in stats]
    total = sum(a * part[1:2] for a, part in zip(scales, stats))
    merged = sum(
        o_all[offset, 0].astype(jnp.float32) * scales[offset] for offset in range(WIDTH)
    )
    write_rows(out_ref, 0, merged, total)


def combine(partial, stats):
    n = partial.shape[1]
    dma = pltpu.SemaphoreType.DMA((WIDTH,))
    return pl.pallas_call(
        combine_body,
        in_specs=[pl.BlockSpec(memory_space=ANY)] * 2,
        out_specs=pl.BlockSpec(memory_space=pltpu.VMEM),
        out_shape=jax.ShapeDtypeStruct((n, NEW, GQ * HD), BF16),
        scratch_shapes=[
            pltpu.VMEM((WIDTH, n, HD, ROWS), BF16),
            pltpu.VMEM((WIDTH, n, 8, ROWS), jnp.float32),
            dma,
            dma,
            dma,
            dma,
            pltpu.SemaphoreType.DMA((2,)),
        ],
        compiler_params=pltpu.CompilerParams(collective_id=1, has_side_effects=True),
        cost_estimate=estimate(n * (24 << 20)),
        name="combine",
    )(partial, stats)


def settle_body(table, *refs):
    out_ref = refs[-1]
    at = 0
    for ref in refs[:-1]:
        for i in range(ref.shape[0]):
            out_ref[table[ORDER + at]] = ref[i]
            at += 1


def settle(table, *parts):
    shape = (SLOTS, NEW, GQ * HD)

    def whole(shape):
        return pl.BlockSpec(shape, lambda i, t: (0, 0, 0))

    return pl.pallas_call(
        settle_body,
        grid_spec=pltpu.PrefetchScalarGridSpec(
            num_scalar_prefetch=1,
            grid=(1,),
            in_specs=[whole(part.shape) for part in parts],
            out_specs=whole(shape),
        ),
        out_shape=jax.ShapeDtypeStruct(shape, BF16),
        cost_estimate=estimate(1 << 20),
        name="settle",
    )(table, *parts)


def matched(branch, run, *args):
    def at(d):
        route = [(g, g ^ d) for g in range(GROUPS)]
        return functools.partial(run, lambda block: lax.ppermute(block, "group", route))

    return lax.switch(branch.reshape(()), [at(d) for d in range(1, GROUPS)], *args)


def shards(
    query, cache_keys, cache_values, new_keys, new_values, masks, movers, block_lists, lengths
):
    query, keys, values = query[0], cache_keys[0], cache_values[0]
    across = lax.ppermute(query, "ctx", [(c, c ^ 1) for c in range(WIDTH)])
    table, *branches = plan(masks, movers, block_lists, lengths)
    pad = ((0, 0), (0, PAD_NEW - OWN_NEW), (0, 0))

    def first(permute, table, payload, query, across, keys, values, new_keys, new_values):
        arrived = permute(payload)
        queries = gather(query, across)
        fresh = jnp.pad(new_keys, pad), jnp.pad(new_values, pad)
        return arrived, queries, *stage(table, keys, values), *fresh

    def second(permute, table, payload, arrived, queries, keys, values, new_keys, new_values):
        now = permute(payload)
        keys, values, ready = renew(table, arrived, keys, values)
        partial = attend(0, 2, table, queries, keys, values, new_keys, new_values)
        return now, ready, reduce(*partial), keys, values

    def third(permute, table, payload, arrived, queries, keys, values, new_keys, new_values):
        now = permute(payload)
        keys, values = unpack(1, table, arrived, keys, values)
        partial = attend(2, 1, table, queries, keys, values, new_keys, new_values)
        return now, reduce(*partial), keys, values

    payload = pack(table, keys, values)
    arrived, queries, keys, values, ready, new_keys, new_values = matched(
        branches[0],
        first,
        table,
        payload,
        query,
        across,
        keys,
        values,
        new_keys[0],
        new_values[0],
    )
    payload = again(1, table, arrived, ready)
    arrived, ready, early, keys, values = matched(
        branches[1], second, table, payload, arrived, queries, keys, values, new_keys, new_values
    )
    payload = again(2, table, arrived, ready)
    arrived, late, keys, values = matched(
        branches[2], third, table, payload, arrived, queries, keys, values, new_keys, new_values
    )
    partial, stats, keys, values = finish(
        table, queries, arrived, new_keys, new_values, keys, values
    )
    attended = settle(table, early, late, combine(partial, stats))
    return (attended[None], keys[None], values[None])


def solution(mesh):
    placed = (
        P("group", None, None, "ctx"),
        P("group", None, "ctx", None),
        P("group", None, "ctx", None),
        P("group", None, "ctx", None),
        P("group", None, "ctx", None),
        P(),
        P(),
        P(),
        P(),
    )
    return jax.shard_map(
        shards,
        mesh=mesh,
        in_specs=placed,
        out_specs=(
            P("group", None, None, "ctx"),
            P("group", None, "ctx", None),
            P("group", None, "ctx", None),
        ),
        check_vma=False,
    )
```

```python
import functools
import math

import jax
import jax.numpy as jnp
from jax import lax
from jax.experimental import pallas as pl
from jax.experimental.pallas import tpu as pltpu
from jax.sharding import PartitionSpec as P

HD = 128
NEW = 32
MATCHINGS = 3
BLOCK = 128
GROUPS = 16
WIDTH = 8
SLOTS = 4
SEG = 512
NB = 4
FEATURES = 1024
GQ = 8
ROWS = GQ * NEW
OWN_NEW = 4
MESH = pl.DeviceIdType.MESH
ANY = pl.ANY
BF16 = jnp.bfloat16
FACTOR = math.log2(math.e) / math.sqrt(HD)
LOWEST = -1e30
FLOOR = -1e29

WHERE = 0
ORDER = 24
VALID = 28
PEERS = 32
FIRST = 40
AGAIN = 41
PAIRS = 52


def peer_at(place, offset):
    x, z = place // 2, place % 2
    return ((x + offset // 2) % 4) * 2 + (z + offset % 2) % 2


def estimate(bytes_accessed, flops=0):
    return pl.CostEstimate(flops=flops, bytes_accessed=bytes_accessed, transcendentals=0)


def plan_body(masks, movers, lists, lengths, table, *branches):
    here = lax.axis_index("group")
    place = lax.axis_index("ctx")
    for m in range(MATCHINGS):
        branches[m][0] = masks[m] - 1
        table[WHERE + 8 * m] = movers[m, here]
        for j in range(NB):
            table[WHERE + 8 * m + 1 + j] = lists[m, j, here]
    second, third = movers[1, here], movers[2, here]

    def rank(s):
        return jnp.where(third == s, 2, jnp.where(second == s, 1, 0))

    for s in range(SLOTS):
        spot = jnp.int32(0)
        for other in range(SLOTS):
            if other != s:
                ahead = rank(other) <= rank(s) if other < s else rank(other) < rank(s)
                spot += ahead.astype(jnp.int32)
        group, slot = here, jnp.int32(s)
        for m in reversed(range(MATCHINGS)):
            moved = movers[m, group] == slot
            group = jnp.where(moved, group ^ masks[m], group)
            slot = jnp.where(moved, movers[m, group], slot)
        table[ORDER + spot] = jnp.int32(s)
        table[VALID + spot] = jnp.clip(lengths[slot, group] - place * SEG, 0, SEG)
    for offset in range(WIDTH):
        table[PEERS + offset] = peer_at(place, offset)
    table[FIRST] = place * OWN_NEW
    for dx in range(WIDTH // 2):
        table[PAIRS + dx] = peer_at(place, 2 * dx) // 2
    for m in range(1, MATCHINGS):
        base = AGAIN + 5 * (m - 1)
        table[base] = (movers[m, here] == movers[m - 1, here]).astype(jnp.int32)
        for j in range(NB):
            spot = jnp.int32(0)
            for i in range(1, NB):
                spot = jnp.where(lists[m - 1, i, here] == lists[m, j, here], i, spot)
            table[base + 1 + j] = spot


def plan(masks, movers, lists, lengths):
    smem = pl.BlockSpec(memory_space=pltpu.SMEM)
    return pl.pallas_call(
        plan_body,
        in_specs=[smem] * 4,
        out_specs=[smem] * 4,
        out_shape=[jax.ShapeDtypeStruct((64,), jnp.int32)]
        + [jax.ShapeDtypeStruct((1,), jnp.int32)] * MATCHINGS,
        name="plan",
    )(masks, movers, jnp.transpose(lists, (0, 2, 1)), jnp.transpose(lengths))


ANYWHERE = pl.BlockSpec(memory_space=ANY)
CACHE = jax.ShapeDtypeStruct((SLOTS, SEG, FEATURES), BF16)
PAYLOAD = jax.ShapeDtypeStruct((2, NB, BLOCK, FEATURES), BF16)
HELD = pltpu.VMEM((NB, 2, BLOCK, FEATURES), BF16)


def in_order(body, start=0, stop=NB):
    def step(j, carry):
        body(j)
        return carry

    lax.fori_loop(start, stop, step, 0)


def copied(src, dst, sem):
    return pltpu.make_async_copy(src, dst, sem)


def block_of(ref, table, matching, j):
    base = WHERE + 8 * matching
    row = pl.multiple_of(table[base + 1 + j] * BLOCK, BLOCK)
    return ref.at[table[base], pl.ds(row, BLOCK)]


def take(matching, table, keys, values, out, held, into, outof):
    def fetch(j, half):
        ref = (keys, values)[half]
        return copied(block_of(ref, table, matching, j), held.at[j, half], into.at[j, half])

    def store(j):
        return copied(held.at[j], out.at[:, j], outof.at[j, 0])

    def start(j):
        fetch(j, 0).start()
        fetch(j, 1).start()

    def turn(j):
        fetch(j, 0).wait()
        fetch(j, 1).wait()
        store(j).start()

    in_order(start)
    in_order(turn)
    in_order(lambda j: store(j).wait())


def put(matching, table, arrived, keys, values, held, into, outof):
    def fetch(j):
        return copied(arrived.at[:, j], held.at[j], into.at[j, 0])

    def store(j, half):
        ref = (keys, values)[half]
        return copied(held.at[j, half], block_of(ref, table, matching, j), outof.at[j, half])

    def turn(j):
        fetch(j).wait()
        store(j, 0).start()
        store(j, 1).start()

    def finish(j):
        store(j, 0).wait()
        store(j, 1).wait()

    in_order(lambda j: fetch(j).start())
    in_order(turn)
    in_order(finish)


def blocks(body, name, n_out, aliases, *args):
    shapes = [CACHE, CACHE] * (n_out // 2) + [PAYLOAD] * (n_out % 2)
    sem = pltpu.SemaphoreType.DMA((NB, 2))
    return pl.pallas_call(
        body,
        grid_spec=pltpu.PrefetchScalarGridSpec(
            num_scalar_prefetch=1,
            grid=(),
            in_specs=[ANYWHERE] * (len(args) - 1),
            out_specs=[ANYWHERE] * n_out,
            scratch_shapes=[HELD, sem, sem],
        ),
        out_shape=shapes,
        input_output_aliases=aliases,
        cost_estimate=estimate(8 << 20),
        name=name,
    )(*args)


def pack(table, keys, values):
    def body(table, keys, values, out, held, into, outof):
        take(0, table, keys, values, out, held, into, outof)

    return blocks(body, "pack", 1, {}, table, keys, values)[0]


def unpack(matching, table, arrived, keys, values):
    def body(table, arrived, keys_in, values_in, keys, values, held, into, outof):
        put(matching, table, arrived, keys, values, held, into, outof)

    return blocks(body, "unpack", 2, {2: 0, 3: 1}, table, arrived, keys, values)


def renew(table, arrived, keys, values):
    def body(table, arrived, keys_in, values_in, keys, values, out, held, into, outof):
        put(0, table, arrived, keys, values, held, into, outof)
        take(2, table, keys, values, out, held, into, outof)

    return blocks(body, "renew", 3, {2: 0, 3: 1}, table, arrived, keys, values)


def again(matching, table, arrived, ready):
    base = AGAIN + 5 * (matching - 1)

    def body(table, arrived, ready, out, held, into, outof):
        def fetch(j):
            return copied(arrived.at[:, table[base + 1 + j]], held.at[j], into.at[j, 0])

        def store(j):
            return copied(held.at[j], out.at[:, j], outof.at[j, 0])

        def turn(j):
            fetch(j).wait()
            store(j).start()

        @pl.when(table[base] == 1)
        def _():
            in_order(lambda j: fetch(j).start())
            in_order(turn)
            in_order(lambda j: store(j).wait())

    return blocks(body, "again", 1, {2: 0}, table, arrived, ready)[0]


def stage_body(table, keys_in, values_in, keys, values, out, k_held, v_held, sem, back, pick):
    def fetch(i, half):
        src, dst = ((keys_in, k_held), (values_in, v_held))[half]
        return copied(src.at[i], dst.at[i], sem.at[i, half])

    def store(i, half):
        src, dst = ((k_held, keys), (v_held, values))[half]
        return copied(src.at[i], dst.at[i], back.at[i, half])

    def select(j, half):
        src = (k_held, v_held)[half]
        return copied(block_of(src, table, 1, j), out.at[half, j], pick.at[j, half])

    def start(i):
        fetch(i, 0).start()
        fetch(i, 1).start()

    def turn(i):
        fetch(i, 0).wait()
        store(i, 0).start()
        fetch(i, 1).wait()
        store(i, 1).start()

    def choose(j):
        select(j, 0).start()
        select(j, 1).start()

    def finish(j):
        select(j, 0).wait()
        select(j, 1).wait()
        store(j, 0).wait()
        store(j, 1).wait()

    in_order(start)
    in_order(turn)
    in_order(choose)
    in_order(finish)


def stage(table, keys, values):
    sem = pltpu.SemaphoreType.DMA((NB, 2))
    held = pltpu.VMEM(CACHE.shape, BF16)
    return pl.pallas_call(
        stage_body,
        grid_spec=pltpu.PrefetchScalarGridSpec(
            num_scalar_prefetch=1,
            grid=(),
            in_specs=[ANYWHERE] * 2,
            out_specs=[ANYWHERE] * 3,
            scratch_shapes=[held, held, sem, sem, sem],
        ),
        out_shape=[CACHE, CACHE, PAYLOAD],
        cost_estimate=estimate(20 << 20),
        name="stage",
    )(table, keys, values)


def gather_body(q_ref, across_ref, out_ref, send, arrive, local):
    group = lax.axis_index("group")
    place = lax.axis_index("ctx")
    x, z = place // 2, place % 2

    def behind(dx):
        return ((x + 4 - dx) % 4) * 2 + z

    barrier = pltpu.get_barrier_semaphore()
    in_order(
        lambda dx: pl.semaphore_signal(
            barrier, inc=1, device_id=(group, behind(dx)), device_id_type=MESH
        ),
        1,
    )
    own = [
        copied(src, out_ref.at[0, half], local.at[half])
        for half, src in enumerate((q_ref, across_ref))
    ]
    for copy in own:
        copy.start()
    for copy in own:
        copy.wait()
    pl.semaphore_wait(barrier, 3)

    def push(dx):
        return pltpu.make_async_remote_copy(
            src_ref=out_ref.at[0],
            dst_ref=out_ref.at[dx],
            send_sem=send.at[dx],
            recv_sem=arrive.at[dx],
            device_id=(group, behind(dx)),
            device_id_type=MESH,
        )

    in_order(lambda dx: push(dx).start(), 1)
    in_order(lambda dx: push(dx).wait(), 1)


def gather(query, across):
    dma = pltpu.SemaphoreType.DMA((WIDTH // 2,))
    pairs = pl.pallas_call(
        gather_body,
        in_specs=[ANYWHERE] * 2,
        out_specs=ANYWHERE,
        out_shape=jax.ShapeDtypeStruct((WIDTH // 2, 2) + query.shape, query.dtype),
        scratch_shapes=[dma, dma, pltpu.SemaphoreType.DMA((2,))],
        compiler_params=pltpu.CompilerParams(collective_id=0, has_side_effects=True),
        cost_estimate=estimate(60 << 20),
        name="gather",
    )(query, across)
    return pairs.reshape((WIDTH,) + query.shape)


CONTRACT_LAST = (((1,), (1,)), ((), ()))
CONTRACT_FIRST = (((0,), (0,)), ((), ()))


def rows_of(q):
    return jnp.concatenate([q[:, g * HD : (g + 1) * HD] for g in range(GQ)], axis=0)


def times(a, b, contract):
    return lax.dot_general(a, b, contract, preferred_element_type=jnp.float32)


def fresh_scores(new_keys, rows, first):
    scores = times(new_keys, rows, CONTRACT_LAST)
    fresh = lax.broadcasted_iota(jnp.int32, scores.shape, 0)
    token = lax.broadcasted_iota(jnp.int32, scores.shape, 1) % NEW
    return jnp.where(first + fresh <= token, scores, LOWEST)


def stats_of(top, total):
    row = lax.broadcasted_iota(jnp.int32, (8, top.shape[1]), 0)
    return jnp.where(row == 0, top, total)


def attend_body(at, n, table, q_ref, keys, values, nk_ref, nv_ref, *rest):
    o_out, s_out, k_held, v_held, o_held, s_held, scores, sem = rest[-8:]
    position = lax.broadcasted_iota(jnp.int32, (SEG, HD), 0)

    def attend_slot(i):
        slot = table[ORDER + at + i]
        count = table[VALID + at + i]
        caches = copied(keys.at[slot], k_held, sem.at[0]), copied(values.at[slot], v_held, sem.at[1])
        sums = (
            copied(o_held, o_out.at[:, at + i], sem.at[2]),
            copied(s_held, s_out.at[:, at + i], sem.at[3]),
        )
        for copy in caches:
            copy.start()
        for copy in caches:
            copy.wait()

        def half(u):
            offset, h = u // 2, u % 2
            head = table[PEERS + offset]
            lanes = pl.ds(pl.multiple_of(head * HD, HD), HD)
            mine = pl.ds(pl.multiple_of(h * HD, HD), HD)
            rows = jnp.concatenate(
                [
                    q_ref[offset, slot, :, pl.ds(pl.multiple_of((h * 4 + g) * HD, HD), HD)]
                    for g in range(4)
                ]
            )
            older = times(k_held[:, lanes], rows, CONTRACT_LAST)
            older = jnp.where(position < count, older, LOWEST)
            newer = fresh_scores(nk_ref[slot, :, lanes], rows, table[FIRST])
            top = jnp.maximum(
                jnp.max(older, axis=0, keepdims=True), jnp.max(newer, axis=0, keepdims=True)
            )
            top = jnp.maximum(top, FLOOR)
            old = jnp.exp2((older - top) * FACTOR)
            new = jnp.exp2((newer - top) * FACTOR)
            total = jnp.sum(old, axis=0, keepdims=True) + jnp.sum(new, axis=0, keepdims=True)
            summed = times(v_held[:, lanes], old.astype(BF16), CONTRACT_FIRST)
            summed += times(nv_ref[slot, :, lanes], new.astype(BF16), CONTRACT_FIRST)
            o_held[head, :, mine] = summed.astype(BF16)
            s_held[head, :, mine] = stats_of(top, total)

        def whole(offset):
            head = table[PEERS + offset]
            lanes = pl.ds(pl.multiple_of(head * HD, HD), HD)
            rows = rows_of(q_ref[offset, slot])
            newer = fresh_scores(nk_ref[slot, :, lanes], rows, table[FIRST])
            within = lax.broadcasted_iota(jnp.int32, (BLOCK, ROWS), 0)

            def chunk(c):
                return pl.ds(pl.multiple_of(c * BLOCK, BLOCK), BLOCK)

            def score(c, top):
                older = times(k_held[chunk(c), lanes], rows, CONTRACT_LAST)
                older = jnp.where(within < count - c * BLOCK, older, LOWEST)
                scores[chunk(c)] = older
                return jnp.maximum(top, jnp.max(older, axis=0, keepdims=True))

            top = jnp.maximum(jnp.max(newer, axis=0, keepdims=True), FLOOR)
            top = lax.fori_loop(0, NB, score, top)

            def weigh(c, sums):
                total, summed = sums
                old = jnp.exp2((scores[chunk(c)] - top) * FACTOR)
                total += jnp.sum(old, axis=0, keepdims=True)
                old = old.astype(BF16)
                return total, summed + times(v_held[chunk(c), lanes], old, CONTRACT_FIRST)

            new = jnp.exp2((newer - top) * FACTOR)
            total = jnp.sum(new, axis=0, keepdims=True)
            summed = times(nv_ref[slot, :, lanes], new.astype(BF16), CONTRACT_FIRST)
            total, summed = lax.fori_loop(0, NB, weigh, (total, summed))
            o_held[head] = summed.astype(BF16)
            s_held[head] = stats_of(top, total)

        if n > 1:
            in_order(whole, 0, WIDTH)
        else:
            in_order(half, 0, 2 * WIDTH)
        for copy in sums:
            copy.start()
        for copy in sums:
            copy.wait()

    in_order(attend_slot, 0, n)


def partials(n):
    return [
        jax.ShapeDtypeStruct((WIDTH, n, HD, ROWS), BF16),
        jax.ShapeDtypeStruct((WIDTH, n, 8, ROWS), jnp.float32),
    ]


def attend(at, n, table, queries, keys, values, new_keys, new_values, *so_far):
    inside = pl.BlockSpec(memory_space=pltpu.VMEM)
    cache = pltpu.VMEM((SEG, FEATURES), BF16)
    return pl.pallas_call(
        functools.partial(attend_body, at, n),
        grid_spec=pltpu.PrefetchScalarGridSpec(
            num_scalar_prefetch=1,
            grid=(),
            in_specs=[inside] + [ANYWHERE] * 2 + [inside] * 2 + [ANYWHERE] * len(so_far),
            out_specs=[ANYWHERE] * 2,
            scratch_shapes=[
                cache,
                cache,
                pltpu.VMEM((WIDTH, HD, ROWS), BF16),
                pltpu.VMEM((WIDTH, 8, ROWS), jnp.float32),
                pltpu.VMEM((SEG, ROWS), jnp.float32),
                pltpu.SemaphoreType.DMA((4,)),
            ],
        ),
        out_shape=partials(SLOTS - 1),
        input_output_aliases={6 + i: i for i in range(len(so_far))},
        cost_estimate=estimate(n * (24 << 20)),
        name="attend",
    )(table, queries, keys, values, new_keys, new_values, *so_far)


def finish_body(
    table, q_ref, arrived, nk_ref, nv_ref, keys_in, values_in, o_ref, s_ref, keys, values, outof
):
    def store(j, half):
        ref = (keys, values)[half]
        return copied(arrived.at[half, j], block_of(ref, table, 2, j), outof.at[j, half])

    for j in range(NB):
        store(j, 0).start()
        store(j, 1).start()
    slot = table[ORDER + SLOTS - 1]
    count = table[VALID + SLOTS - 1]
    within = lax.broadcasted_iota(jnp.int32, (BLOCK, ROWS), 0)
    starts = [table[WHERE + 16 + 1 + j] * BLOCK for j in range(NB)]

    def pair(dx):
        for offset in range(2):
            head = table[PEERS + 2 * dx + offset]
            lanes = pl.ds(pl.multiple_of(head * HD, HD), HD)
            rows = rows_of(q_ref[2 * dx + offset, slot])
            newer = fresh_scores(nk_ref[slot, :, lanes], rows, table[FIRST])
            older = times(
                arrived[0, :, :, lanes].reshape(SEG, HD), rows, CONTRACT_LAST
            )
            older = jnp.concatenate(
                [
                    jnp.where(
                        within < count - starts[j], older[j * BLOCK : (j + 1) * BLOCK], LOWEST
                    )
                    for j in range(NB)
                ]
            )
            top = jnp.maximum(
                jnp.max(older, axis=0, keepdims=True), jnp.max(newer, axis=0, keepdims=True)
            )
            top = jnp.maximum(top, FLOOR)
            old = jnp.exp2((older - top) * FACTOR)
            new = jnp.exp2((newer - top) * FACTOR)
            total = jnp.sum(old, axis=0, keepdims=True) + jnp.sum(new, axis=0, keepdims=True)
            summed = times(
                arrived[1, :, :, lanes].reshape(SEG, HD), old.astype(BF16), CONTRACT_FIRST
            )
            summed += times(nv_ref[slot, :, lanes], new.astype(BF16), CONTRACT_FIRST)
            o_ref[head, 0] = summed.astype(BF16)
            s_ref[head, 0] = stats_of(top, total)

    in_order(pair, 0, WIDTH // 2)
    for j in range(NB):
        store(j, 0).wait()
        store(j, 1).wait()


def finish(table, queries, arrived, new_keys, new_values, keys, values):
    inside = pl.BlockSpec(memory_space=pltpu.VMEM)
    return pl.pallas_call(
        finish_body,
        grid_spec=pltpu.PrefetchScalarGridSpec(
            num_scalar_prefetch=1,
            grid=(),
            in_specs=[inside] * 4 + [ANYWHERE] * 2,
            out_specs=[inside] * 2 + [ANYWHERE] * 2,
            scratch_shapes=[pltpu.SemaphoreType.DMA((NB, 2))],
        ),
        out_shape=partials(1) + [CACHE, CACHE],
        input_output_aliases={5: 2, 6: 3},
        cost_estimate=estimate(24 << 20),
        name="finish",
    )(table, queries, arrived, new_keys, new_values, keys, values)


def fold(shares, read_top, read_total, read_sum):
    top = lax.fori_loop(1, shares, lambda j, t: jnp.maximum(t, read_top(j)), read_top(0))

    def add(j, sums):
        total, merged = sums
        scale = jnp.exp2((read_top(j) - top) * FACTOR)
        return total + scale * read_total(j), merged + read_sum(j) * scale

    zero = (jnp.zeros((1, ROWS), jnp.float32), jnp.zeros((HD, ROWS), jnp.float32))
    return (top,) + lax.fori_loop(0, shares, add, zero)


def write_rows(out_ref, i, merged):
    rows = jnp.transpose(merged)
    for g in range(GQ):
        out_ref[i, :, g * HD : (g + 1) * HD] = rows[g * NEW : (g + 1) * NEW].astype(BF16)


def reduce_body(
    n, o_ref, s_ref, out_ref, o_all, s_all, o_mid, s_mid, o_in, s_in, send, arrive, local
):
    group = lax.axis_index("group")
    place = lax.axis_index("ctx")
    x, z = place // 2, place % 2
    across = x * 2 + (z + 1) % 2

    def pair_at(dx):
        return pl.ds(2 * ((x + dx) % 4), 2)

    def push(dx, half):
        src, dst = ((o_ref, o_all), (s_ref, s_all))[half]
        return pltpu.make_async_remote_copy(
            src_ref=src.at[pair_at(dx)],
            dst_ref=dst.at[dx],
            send_sem=send.at[dx, half],
            recv_sem=arrive.at[dx, half],
            device_id=(group, ((x + dx) % 4) * 2 + z),
            device_id_type=MESH,
        )

    def swap(half):
        src, dst = ((o_mid, o_in), (s_mid, s_in))[half]
        return pltpu.make_async_remote_copy(
            src_ref=src.at[0],
            dst_ref=dst,
            send_sem=send.at[0, half],
            recv_sem=arrive.at[0, half],
            device_id=(group, across),
            device_id_type=MESH,
        )

    def own(half):
        src, dst = ((o_ref, o_all), (s_ref, s_all))[half]
        return copied(src.at[pair_at(0)], dst.at[0], local.at[half])

    def start(dx):
        push(dx, 0).start()
        push(dx, 1).start()

    def done(dx):
        push(dx, 0).wait()
        push(dx, 1).wait()

    barrier = pltpu.get_barrier_semaphore()
    in_order(
        lambda dx: pl.semaphore_signal(
            barrier, inc=1, device_id=(group, ((x + dx) % 4) * 2 + z), device_id_type=MESH
        ),
        1,
    )
    pl.semaphore_signal(barrier, inc=1, device_id=(group, across), device_id_type=MESH)
    own(0).start()
    own(1).start()
    pl.semaphore_wait(barrier, 4)
    in_order(start, 1)
    own(0).wait()
    own(1).wait()
    in_order(done, 1)

    def part(k):
        whose = (z + 1 + k) % 2

        def slot(i):
            top, total, merged = fold(
                4,
                lambda j: s_all[j, whose, i, 0:1],
                lambda j: s_all[j, whose, i, 1:2],
                lambda j: o_all[j, whose, i].astype(jnp.float32),
            )
            o_mid[k, i] = merged
            s_mid[k, i] = stats_of(top, total)

        in_order(slot, 0, n)

    in_order(part, 0, 2)
    swap(0).start()
    swap(1).start()
    swap(0).wait()
    swap(1).wait()

    def join(i):
        left, right = s_mid[1, i], s_in[i]
        top = jnp.maximum(left[0:1], right[0:1])
        a = jnp.exp2((left[0:1] - top) * FACTOR)
        b = jnp.exp2((right[0:1] - top) * FACTOR)
        total = a * left[1:2] + b * right[1:2]
        out_ref[i] = (o_mid[1, i] * a + o_in[i] * b) / total

    in_order(join, 0, n)


def reduce(partial, stats):
    n = partial.shape[1]
    dma = pltpu.SemaphoreType.DMA((4, 2))
    return pl.pallas_call(
        functools.partial(reduce_body, n),
        in_specs=[ANYWHERE] * 2,
        out_specs=pl.BlockSpec(memory_space=pltpu.VMEM),
        out_shape=jax.ShapeDtypeStruct((n, HD, ROWS), jnp.float32),
        scratch_shapes=[
            pltpu.VMEM((4, 2, n, HD, ROWS), BF16),
            pltpu.VMEM((4, 2, n, 8, ROWS), jnp.float32),
            pltpu.VMEM((2, n, HD, ROWS), jnp.float32),
            pltpu.VMEM((2, n, 8, ROWS), jnp.float32),
            pltpu.VMEM((n, HD, ROWS), jnp.float32),
            pltpu.VMEM((n, 8, ROWS), jnp.float32),
            dma,
            dma,
            pltpu.SemaphoreType.DMA((2,)),
        ],
        compiler_params=pltpu.CompilerParams(collective_id=2, has_side_effects=True),
        cost_estimate=estimate(n * (24 << 20)),
        name="reduce",
    )(partial, stats)


def combine_body(o_ref, s_ref, out_ref, o_all, s_all, sem_o, sem_s, arrive_o, arrive_s, local):
    group = lax.axis_index("group")
    place = lax.axis_index("ctx")
    barrier = pltpu.get_barrier_semaphore()
    for offset in range(1, WIDTH):
        pl.semaphore_signal(
            barrier, inc=1, device_id=(group, peer_at(place, offset)), device_id_type=MESH
        )
    own_o = pltpu.make_async_copy(o_ref.at[place], o_all.at[0], local.at[0])
    own_s = pltpu.make_async_copy(s_ref.at[place], s_all.at[0], local.at[1])
    own_o.start()
    own_s.start()
    pl.semaphore_wait(barrier, WIDTH - 1)
    sends = []
    for offset in (4, 5, 2, 6, 3, 7, 1):
        peer = peer_at(place, offset)
        for src, dst, send, recv in (
            (o_ref, o_all, sem_o, arrive_o),
            (s_ref, s_all, sem_s, arrive_s),
        ):
            copy = pltpu.make_async_remote_copy(
                src_ref=src.at[peer],
                dst_ref=dst.at[offset],
                send_sem=send.at[offset],
                recv_sem=recv.at[offset],
                device_id=(group, peer),
                device_id_type=MESH,
            )
            copy.start()
            sends.append(copy)
    own_o.wait()
    own_s.wait()
    for copy in sends:
        copy.wait()
    stats = [s_all[offset, 0] for offset in range(WIDTH)]
    top = functools.reduce(jnp.maximum, [part[0:1] for part in stats])
    scales = [jnp.exp2((part[0:1] - top) * FACTOR) for part in stats]
    total = sum(a * part[1:2] for a, part in zip(scales, stats))
    merged = sum(
        o_all[offset, 0].astype(jnp.float32) * scales[offset] for offset in range(WIDTH)
    )
    write_rows(out_ref, 0, merged / total)


def combine(partial, stats):
    n = partial.shape[1]
    dma = pltpu.SemaphoreType.DMA((WIDTH,))
    return pl.pallas_call(
        combine_body,
        in_specs=[pl.BlockSpec(memory_space=ANY)] * 2,
        out_specs=pl.BlockSpec(memory_space=pltpu.VMEM),
        out_shape=jax.ShapeDtypeStruct((n, NEW, GQ * HD), BF16),
        scratch_shapes=[
            pltpu.VMEM((WIDTH, n, HD, ROWS), BF16),
            pltpu.VMEM((WIDTH, n, 8, ROWS), jnp.float32),
            dma,
            dma,
            dma,
            dma,
            pltpu.SemaphoreType.DMA((2,)),
        ],
        compiler_params=pltpu.CompilerParams(collective_id=1, has_side_effects=True),
        cost_estimate=estimate(n * (24 << 20)),
        name="combine",
    )(partial, stats)


def settle_body(table, early, last, out_ref):
    def place(i):
        write_rows(out_ref, table[ORDER + i], early[i])

    in_order(place, 0, SLOTS - 1)
    out_ref[table[ORDER + SLOTS - 1]] = last[0]


def settle(table, early, last):
    shape = (SLOTS, NEW, GQ * HD)
    inside = pl.BlockSpec(memory_space=pltpu.VMEM)
    return pl.pallas_call(
        settle_body,
        grid_spec=pltpu.PrefetchScalarGridSpec(
            num_scalar_prefetch=1, grid=(), in_specs=[inside] * 2, out_specs=inside
        ),
        out_shape=jax.ShapeDtypeStruct(shape, BF16),
        cost_estimate=estimate(1 << 20),
        name="settle",
    )(table, early, last)


def matched(branch, run, *args):
    def at(d):
        route = [(g, g ^ d) for g in range(GROUPS)]
        return functools.partial(run, lambda block: lax.ppermute(block, "group", route))

    return lax.switch(branch.reshape(()), [at(d) for d in range(1, GROUPS)], *args)


def shards(
    query, cache_keys, cache_values, new_keys, new_values, masks, movers, block_lists, lengths
):
    query, keys, values = query[0], cache_keys[0], cache_values[0]
    across = lax.ppermute(query, "ctx", [(c, c ^ 1) for c in range(WIDTH)])
    table, *branches = plan(masks, movers, block_lists, lengths)
    new_keys, new_values = new_keys[0], new_values[0]

    def first(permute, table, payload, query, across, keys, values):
        arrived = permute(payload)
        return arrived, gather(query, across), *stage(table, keys, values)

    def second(permute, table, payload, arrived, queries, keys, values, new_keys, new_values):
        now = permute(payload)
        keys, values, ready = renew(table, arrived, keys, values)
        partial = attend(0, 2, table, queries, keys, values, new_keys, new_values)
        return now, ready, keys, values, *partial

    def third(
        permute, table, payload, arrived, queries, keys, values, new_keys, new_values, *partial
    ):
        now = permute(payload)
        keys, values = unpack(1, table, arrived, keys, values)
        partial = attend(2, 1, table, queries, keys, values, new_keys, new_values, *partial)
        return now, keys, values, reduce(*partial)

    payload = pack(table, keys, values)
    arrived, queries, keys, values, ready = matched(
        branches[0], first, table, payload, query, across, keys, values
    )
    payload = again(1, table, arrived, ready)
    state = (queries, keys, values, new_keys, new_values)
    arrived, ready, keys, values, *partial = matched(
        branches[1], second, table, payload, arrived, *state
    )
    payload = again(2, table, arrived, ready)
    state = (queries, keys, values, new_keys, new_values)
    arrived, keys, values, early = matched(
        branches[2], third, table, payload, arrived, *state, *partial
    )
    partial, stats, keys, values = finish(
        table, queries, arrived, new_keys, new_values, keys, values
    )
    attended = settle(table, early, combine(partial, stats))
    return (attended[None], keys[None], values[None])


def solution(mesh):
    placed = (
        P("group", None, None, "ctx"),
        P("group", None, "ctx", None),
        P("group", None, "ctx", None),
        P("group", None, "ctx", None),
        P("group", None, "ctx", None),
        P(),
        P(),
        P(),
        P(),
    )
    return jax.shard_map(
        shards,
        mesh=mesh,
        in_specs=placed,
        out_specs=(
            P("group", None, None, "ctx"),
            P("group", None, "ctx", None),
            P("group", None, "ctx", None),
        ),
        check_vma=False,
    )
```

```python
import functools
import math

import jax
import jax.numpy as jnp
from jax import lax
from jax.experimental import pallas as pl
from jax.experimental.pallas import tpu as pltpu
from jax.sharding import PartitionSpec as P

HD = 128
NEW = 32
MATCHINGS = 3
BLOCK = 128
GROUPS = 16
WIDTH = 8
SLOTS = 4
SEG = 512
NB = 4
FEATURES = 1024
GQ = 8
ROWS = GQ * NEW
OWN_NEW = 4
MESH = pl.DeviceIdType.MESH
ANY = pl.ANY
BF16 = jnp.bfloat16
FACTOR = math.log2(math.e) / math.sqrt(HD)
LOWEST = -1e30
FLOOR = -1e29

WHERE = 0
ORDER = 24
VALID = 28
PEERS = 32
FIRST = 40
AGAIN = 41
PAIRS = 52


def peer_at(place, offset):
    x, z = place // 2, place % 2
    return ((x + offset // 2) % 4) * 2 + (z + offset % 2) % 2


def estimate(bytes_accessed, flops=0):
    return pl.CostEstimate(flops=flops, bytes_accessed=bytes_accessed, transcendentals=0)


def plan_body(masks, movers, lists, lengths, table, branches):
    here = lax.axis_index("group")
    place = lax.axis_index("ctx")
    for m in range(MATCHINGS):
        branches[m][0] = masks[m] - 1
        table[WHERE + 8 * m] = movers[m, here]
        for j in range(NB):
            table[WHERE + 8 * m + 1 + j] = lists[m, j, here]
    second, third = movers[1, here], movers[2, here]

    def rank(s):
        return jnp.where(third == s, 2, jnp.where(second == s, 1, 0))

    for s in range(SLOTS):
        spot = jnp.int32(0)
        for other in range(SLOTS):
            if other != s:
                ahead = rank(other) <= rank(s) if other < s else rank(other) < rank(s)
                spot += ahead.astype(jnp.int32)
        group, slot = here, jnp.int32(s)
        for m in reversed(range(MATCHINGS)):
            moved = movers[m, group] == slot
            group = jnp.where(moved, group ^ masks[m], group)
            slot = jnp.where(moved, movers[m, group], slot)
        table[ORDER + spot] = jnp.int32(s)
        table[VALID + spot] = jnp.clip(lengths[slot, group] - place * SEG, 0, SEG)
    for offset in range(WIDTH):
        table[PEERS + offset] = peer_at(place, offset)
    table[FIRST] = place * OWN_NEW
    for dx in range(WIDTH // 2):
        table[PAIRS + dx] = peer_at(place, 2 * dx) // 2
    for m in range(1, MATCHINGS):
        base = AGAIN + 5 * (m - 1)
        table[base] = (movers[m, here] == movers[m - 1, here]).astype(jnp.int32)
        for j in range(NB):
            spot = jnp.int32(0)
            for i in range(1, NB):
                spot = jnp.where(lists[m - 1, i, here] == lists[m, j, here], i, spot)
            table[base + 1 + j] = spot


ANYWHERE = pl.BlockSpec(memory_space=ANY)
CACHE = jax.ShapeDtypeStruct((SLOTS, SEG, FEATURES), BF16)
PAYLOAD = jax.ShapeDtypeStruct((2, NB, BLOCK, FEATURES), BF16)
HELD = pltpu.VMEM((NB, 2, BLOCK, FEATURES), BF16)


def in_order(body, start=0, stop=NB):
    def step(j, carry):
        body(j)
        return carry

    lax.fori_loop(start, stop, step, 0)


def copied(src, dst, sem):
    return pltpu.make_async_copy(src, dst, sem)


def block_of(ref, table, matching, j):
    base = WHERE + 8 * matching
    row = pl.multiple_of(table[base + 1 + j] * BLOCK, BLOCK)
    return ref.at[table[base], pl.ds(row, BLOCK)]


def take(matching, table, keys, values, out, held, into, outof):
    def fetch(j, half):
        ref = (keys, values)[half]
        return copied(block_of(ref, table, matching, j), held.at[j, half], into.at[j, half])

    def store(j):
        return copied(held.at[j], out.at[:, j], outof.at[j, 0])

    def start(j):
        fetch(j, 0).start()
        fetch(j, 1).start()

    def turn(j):
        fetch(j, 0).wait()
        fetch(j, 1).wait()
        store(j).start()

    in_order(start)
    in_order(turn)
    in_order(lambda j: store(j).wait())


def put(matching, table, arrived, keys, values, held, into, outof, meanwhile=None):
    def fetch(j):
        return copied(arrived.at[:, j], held.at[j], into.at[j, 0])

    def store(j, half):
        ref = (keys, values)[half]
        return copied(held.at[j, half], block_of(ref, table, matching, j), outof.at[j, half])

    def turn(j):
        fetch(j).wait()
        store(j, 0).start()
        store(j, 1).start()

    def finish(j):
        store(j, 0).wait()
        store(j, 1).wait()

    in_order(lambda j: fetch(j).start())
    in_order(turn)
    if meanwhile:
        meanwhile()
    in_order(finish)


def blocks(body, name, n_out, aliases, *args):
    shapes = [CACHE, CACHE] * (n_out // 2) + [PAYLOAD] * (n_out % 2)
    sem = pltpu.SemaphoreType.DMA((NB, 2))
    return pl.pallas_call(
        body,
        grid_spec=pltpu.PrefetchScalarGridSpec(
            num_scalar_prefetch=1,
            grid=(),
            in_specs=[ANYWHERE] * (len(args) - 1),
            out_specs=[ANYWHERE] * n_out,
            scratch_shapes=[HELD, sem, sem],
        ),
        out_shape=shapes,
        input_output_aliases=aliases,
        cost_estimate=estimate(8 << 20),
        name=name,
    )(*args)


def begin_body(masks, movers, lists, lengths, keys, values, *rest):
    *branches, table, out, held, into, outof = rest
    plan_body(masks, movers, lists, lengths, table, branches)
    take(0, table, keys, values, out, held, into, outof)


def begin(masks, movers, lists, lengths, keys, values):
    smem = pl.BlockSpec(memory_space=pltpu.SMEM)
    sem = pltpu.SemaphoreType.DMA((NB, 2))
    return pl.pallas_call(
        begin_body,
        in_specs=[smem] * 4 + [ANYWHERE] * 2,
        out_specs=[smem] * 4 + [ANYWHERE],
        out_shape=[jax.ShapeDtypeStruct((1,), jnp.int32)] * MATCHINGS
        + [jax.ShapeDtypeStruct((64,), jnp.int32), PAYLOAD],
        scratch_shapes=[HELD, sem, sem],
        name="begin",
    )(masks, movers, jnp.transpose(lists, (0, 2, 1)), jnp.transpose(lengths), keys, values)


def unpack(matching, table, arrived, keys, values):
    def body(table, arrived, keys_in, values_in, keys, values, held, into, outof):
        put(matching, table, arrived, keys, values, held, into, outof)

    return blocks(body, "unpack", 2, {2: 0, 3: 1}, table, arrived, keys, values)


def renew(table, arrived, keys, values):
    def body(table, arrived, keys_in, values_in, keys, values, out, held, into, outof):
        put(0, table, arrived, keys, values, held, into, outof)
        take(2, table, keys, values, out, held, into, outof)

    return blocks(body, "renew", 3, {2: 0, 3: 1}, table, arrived, keys, values)


def again(matching, table, arrived, ready):
    base = AGAIN + 5 * (matching - 1)

    def body(table, arrived, ready, out, held, into, outof):
        def fetch(j):
            return copied(arrived.at[:, table[base + 1 + j]], held.at[j], into.at[j, 0])

        def store(j):
            return copied(held.at[j], out.at[:, j], outof.at[j, 0])

        def turn(j):
            fetch(j).wait()
            store(j).start()

        @pl.when(table[base] == 1)
        def _():
            in_order(lambda j: fetch(j).start())
            in_order(turn)
            in_order(lambda j: store(j).wait())

    return blocks(body, "again", 1, {2: 0}, table, arrived, ready)[0]


def stage_body(table, keys_in, values_in, keys, values, out, k_held, v_held, sem, back, pick):
    def fetch(i, half):
        src, dst = ((keys_in, k_held), (values_in, v_held))[half]
        return copied(src.at[i], dst.at[i], sem.at[i, half])

    def store(i, half):
        src, dst = ((k_held, keys), (v_held, values))[half]
        return copied(src.at[i], dst.at[i], back.at[i, half])

    def select(j, half):
        src = (k_held, v_held)[half]
        return copied(block_of(src, table, 1, j), out.at[half, j], pick.at[j, half])

    def start(i):
        fetch(i, 0).start()
        fetch(i, 1).start()

    def turn(i):
        fetch(i, 0).wait()
        store(i, 0).start()
        fetch(i, 1).wait()
        store(i, 1).start()

    def choose(j):
        select(j, 0).start()
        select(j, 1).start()

    def finish(j):
        select(j, 0).wait()
        select(j, 1).wait()
        store(j, 0).wait()
        store(j, 1).wait()

    in_order(start)
    in_order(turn)
    in_order(choose)
    in_order(finish)


def stage(table, keys, values):
    sem = pltpu.SemaphoreType.DMA((NB, 2))
    held = pltpu.VMEM(CACHE.shape, BF16)
    return pl.pallas_call(
        stage_body,
        grid_spec=pltpu.PrefetchScalarGridSpec(
            num_scalar_prefetch=1,
            grid=(),
            in_specs=[ANYWHERE] * 2,
            out_specs=[ANYWHERE] * 3,
            scratch_shapes=[held, held, sem, sem, sem],
        ),
        out_shape=[CACHE, CACHE, PAYLOAD],
        cost_estimate=estimate(20 << 20),
        name="stage",
    )(table, keys, values)


def gather_body(q_ref, across_ref, out_ref, send, arrive, local):
    group = lax.axis_index("group")
    place = lax.axis_index("ctx")
    x, z = place // 2, place % 2

    def behind(dx):
        return ((x + 4 - dx) % 4) * 2 + z

    barrier = pltpu.get_barrier_semaphore()
    in_order(
        lambda dx: pl.semaphore_signal(
            barrier, inc=1, device_id=(group, behind(dx)), device_id_type=MESH
        ),
        1,
    )
    own = [
        copied(src, out_ref.at[0, half], local.at[half])
        for half, src in enumerate((q_ref, across_ref))
    ]
    for copy in own:
        copy.start()
    for copy in own:
        copy.wait()
    pl.semaphore_wait(barrier, 3)

    def push(dx):
        return pltpu.make_async_remote_copy(
            src_ref=out_ref.at[0],
            dst_ref=out_ref.at[dx],
            send_sem=send.at[dx],
            recv_sem=arrive.at[dx],
            device_id=(group, behind(dx)),
            device_id_type=MESH,
        )

    in_order(lambda dx: push(dx).start(), 1)
    in_order(lambda dx: push(dx).wait(), 1)


def gather(query, across):
    dma = pltpu.SemaphoreType.DMA((WIDTH // 2,))
    pairs = pl.pallas_call(
        gather_body,
        in_specs=[ANYWHERE] * 2,
        out_specs=ANYWHERE,
        out_shape=jax.ShapeDtypeStruct((WIDTH // 2, 2) + query.shape, query.dtype),
        scratch_shapes=[dma, dma, pltpu.SemaphoreType.DMA((2,))],
        compiler_params=pltpu.CompilerParams(collective_id=0, has_side_effects=True),
        cost_estimate=estimate(60 << 20),
        name="gather",
    )(query, across)
    return pairs.reshape((WIDTH,) + query.shape)


CONTRACT_LAST = (((1,), (1,)), ((), ()))
CONTRACT_FIRST = (((0,), (0,)), ((), ()))


def rows_of(q):
    return jnp.concatenate([q[:, g * HD : (g + 1) * HD] for g in range(GQ)], axis=0)


def times(a, b, contract):
    return lax.dot_general(a, b, contract, preferred_element_type=jnp.float32)


def fresh_scores(new_keys, rows, first):
    scores = times(new_keys, rows, CONTRACT_LAST)
    fresh = lax.broadcasted_iota(jnp.int32, scores.shape, 0)
    token = lax.broadcasted_iota(jnp.int32, scores.shape, 1) % NEW
    return jnp.where(first + fresh <= token, scores, LOWEST)


def stats_of(top, total):
    row = lax.broadcasted_iota(jnp.int32, (8, top.shape[1]), 0)
    return jnp.where(row == 0, top, total)


def attend_body(at, n, steps, table, q_ref, keys, values, nk_ref, nv_ref, *rest):
    o_out, s_out, k_held, v_held, o_held, s_held, scores, sem = rest[-8:]
    size = SEG // steps
    within = lax.broadcasted_iota(jnp.int32, (size, ROWS), 0)

    def attend_slot(i):
        slot = table[ORDER + at + i]
        count = table[VALID + at + i]
        caches = copied(keys.at[slot], k_held, sem.at[0]), copied(values.at[slot], v_held, sem.at[1])
        sums = (
            copied(o_held, o_out.at[:, at + i], sem.at[2]),
            copied(s_held, s_out.at[:, at + i], sem.at[3]),
        )
        for copy in caches:
            copy.start()
        for copy in caches:
            copy.wait()

        def whole(offset):
            head = table[PEERS + offset]
            lanes = pl.ds(pl.multiple_of(head * HD, HD), HD)
            rows = rows_of(q_ref[offset, slot])
            newer = fresh_scores(nk_ref[slot, :, lanes], rows, table[FIRST])

            def chunk(c):
                return pl.ds(pl.multiple_of(c * size, size), size)

            def score(c, top):
                older = times(k_held[chunk(c), lanes], rows, CONTRACT_LAST)
                older = jnp.where(within < count - c * size, older, LOWEST)
                scores[chunk(c)] = older
                return jnp.maximum(top, jnp.max(older, axis=0, keepdims=True))

            top = jnp.maximum(jnp.max(newer, axis=0, keepdims=True), FLOOR)
            top = lax.fori_loop(0, steps, score, top)

            def weigh(c, sums):
                total, summed = sums
                old = jnp.exp2((scores[chunk(c)] - top) * FACTOR)
                total += jnp.sum(old, axis=0, keepdims=True)
                old = old.astype(BF16)
                return total, summed + times(v_held[chunk(c), lanes], old, CONTRACT_FIRST)

            new = jnp.exp2((newer - top) * FACTOR)
            total = jnp.sum(new, axis=0, keepdims=True)
            summed = times(nv_ref[slot, :, lanes], new.astype(BF16), CONTRACT_FIRST)
            total, summed = lax.fori_loop(0, steps, weigh, (total, summed))
            o_held[head] = summed.astype(BF16)
            s_held[head] = stats_of(top, total)

        in_order(whole, 0, WIDTH)
        for copy in sums:
            copy.start()
        for copy in sums:
            copy.wait()

    in_order(attend_slot, 0, n)


def partials(n):
    return [
        jax.ShapeDtypeStruct((WIDTH, n, HD, ROWS), BF16),
        jax.ShapeDtypeStruct((WIDTH, n, 8, ROWS), jnp.float32),
    ]


def attend(at, n, steps, table, queries, keys, values, new_keys, new_values, *so_far):
    inside = pl.BlockSpec(memory_space=pltpu.VMEM)
    cache = pltpu.VMEM((SEG, FEATURES), BF16)
    return pl.pallas_call(
        functools.partial(attend_body, at, n, steps),
        grid_spec=pltpu.PrefetchScalarGridSpec(
            num_scalar_prefetch=1,
            grid=(),
            in_specs=[inside] + [ANYWHERE] * 2 + [inside] * 2 + [ANYWHERE] * len(so_far),
            out_specs=[ANYWHERE] * 2,
            scratch_shapes=[
                cache,
                cache,
                pltpu.VMEM((WIDTH, HD, ROWS), BF16),
                pltpu.VMEM((WIDTH, 8, ROWS), jnp.float32),
                pltpu.VMEM((SEG, ROWS), jnp.float32),
                pltpu.SemaphoreType.DMA((4,)),
            ],
        ),
        out_shape=partials(SLOTS - 1),
        input_output_aliases={6 + i: i for i in range(len(so_far))},
        cost_estimate=estimate(n * (24 << 20)),
        name="attend",
    )(table, queries, keys, values, new_keys, new_values, *so_far)


def fold(shares, read_top, read_total, read_sum):
    top = lax.fori_loop(1, shares, lambda j, t: jnp.maximum(t, read_top(j)), read_top(0))

    def add(j, sums):
        total, merged = sums
        scale = jnp.exp2((read_top(j) - top) * FACTOR)
        return total + scale * read_total(j), merged + read_sum(j) * scale

    zero = (jnp.zeros((1, ROWS), jnp.float32), jnp.zeros((HD, ROWS), jnp.float32))
    return (top,) + lax.fori_loop(0, shares, add, zero)


def write_rows(out_ref, i, merged):
    rows = jnp.transpose(merged)
    for g in range(GQ):
        out_ref[i, :, g * HD : (g + 1) * HD] = rows[g * NEW : (g + 1) * NEW].astype(BF16)


def reduce_body(
    n, o_ref, s_ref, out_ref, o_all, s_all, o_own, s_mid, o_mid, o_in, s_in, send, arrive, local
):
    group = lax.axis_index("group")
    place = lax.axis_index("ctx")
    x, z = place // 2, place % 2
    across = x * 2 + (z + 1) % 2

    def pair_at(dx):
        return pl.ds(2 * ((x + dx) % 4), 2)

    def remote(src, dst, row, column, peer):
        return pltpu.make_async_remote_copy(
            src_ref=src,
            dst_ref=dst,
            send_sem=send.at[row, column],
            recv_sem=arrive.at[row, column],
            device_id=(group, peer),
            device_id_type=MESH,
        )

    def behind(dx):
        return ((x + dx) % 4) * 2 + z

    def push(i, dx):
        return remote(o_ref.at[pair_at(dx), i], o_all.at[i, dx], i, dx, behind(dx))

    def push_stats(dx):
        return remote(s_ref.at[pair_at(dx)], s_all.at[dx], n, dx, behind(dx))

    def swap(i):
        return remote(o_mid.at[i], o_in.at[i], i, 0, across)

    def swap_stats(i):
        return remote(s_mid.at[0, i], s_in.at[i], i, 4, across)

    own_s = copied(s_ref.at[pair_at(0)], s_all.at[0], local.at[n])

    def own(i):
        return copied(o_ref.at[pair_at(0), i], o_all.at[i, 0], local.at[i])

    barrier = pltpu.get_barrier_semaphore()
    in_order(
        lambda dx: pl.semaphore_signal(
            barrier, inc=1, device_id=(group, behind(dx)), device_id_type=MESH
        ),
        1,
    )
    pl.semaphore_signal(barrier, inc=1, device_id=(group, across), device_id_type=MESH)
    own_s.start()
    in_order(lambda i: own(i).start(), 0, n)
    pl.semaphore_wait(barrier, 4)
    in_order(lambda dx: push_stats(dx).start(), 1)
    in_order(lambda i: in_order(lambda dx: push(i, dx).start(), 1), 0, n)
    own_s.wait()
    in_order(lambda dx: push_stats(dx).wait(), 1)

    def slot(i):
        own(i).wait()
        in_order(lambda dx: push(i, dx).wait(), 1)

        def part(k):
            whose = (z + 1 + k) % 2
            top, total, merged = fold(
                4,
                lambda j: s_all[j, whose, i, 0:1],
                lambda j: s_all[j, whose, i, 1:2],
                lambda j: o_all[i, j, whose].astype(jnp.float32),
            )
            o_own[i] = merged
            s_mid[k, i] = stats_of(top, total)

            @pl.when(k == 0)
            def _():
                o_mid[i] = merged.astype(BF16)

        in_order(part, 0, 2)
        swap(i).start()
        swap_stats(i).start()

    in_order(slot, 0, n)

    def join(i):
        swap(i).wait()
        swap_stats(i).wait()
        left, right = s_mid[1, i], s_in[i]
        top = jnp.maximum(left[0:1], right[0:1])
        a = jnp.exp2((left[0:1] - top) * FACTOR)
        b = jnp.exp2((right[0:1] - top) * FACTOR)
        total = a * left[1:2] + b * right[1:2]
        out_ref[i] = (o_own[i] * a + o_in[i].astype(jnp.float32) * b) / total

    in_order(join, 0, n)


def reduce(partial, stats):
    n = partial.shape[1]
    dma = pltpu.SemaphoreType.DMA((n + 1, 5))
    return pl.pallas_call(
        functools.partial(reduce_body, n),
        in_specs=[ANYWHERE] * 2,
        out_specs=pl.BlockSpec(memory_space=pltpu.VMEM),
        out_shape=jax.ShapeDtypeStruct((n, HD, ROWS), jnp.float32),
        scratch_shapes=[
            pltpu.VMEM((n, 4, 2, HD, ROWS), BF16),
            pltpu.VMEM((4, 2, n, 8, ROWS), jnp.float32),
            pltpu.VMEM((n, HD, ROWS), jnp.float32),
            pltpu.VMEM((2, n, 8, ROWS), jnp.float32),
            pltpu.VMEM((n, HD, ROWS), BF16),
            pltpu.VMEM((n, HD, ROWS), BF16),
            pltpu.VMEM((n, 8, ROWS), jnp.float32),
            dma,
            dma,
            pltpu.SemaphoreType.DMA((n + 1,)),
        ],
        compiler_params=pltpu.CompilerParams(collective_id=2, has_side_effects=True),
        cost_estimate=estimate(n * (24 << 20)),
        name="reduce",
    )(partial, stats)


def close_body(
    table, q_ref, arrived, nk_ref, nv_ref, out_ref, o_held, s_held, o_all, s_all, send, arrive
):
    group = lax.axis_index("group")
    place = lax.axis_index("ctx")
    barrier = pltpu.get_barrier_semaphore()
    for offset in range(1, WIDTH):
        pl.semaphore_signal(
            barrier, inc=1, device_id=(group, peer_at(place, offset)), device_id_type=MESH
        )
    slot = table[ORDER + SLOTS - 1]
    count = table[VALID + SLOTS - 1]
    within = lax.broadcasted_iota(jnp.int32, (BLOCK, ROWS), 0)
    starts = [table[WHERE + 16 + 1 + j] * BLOCK for j in range(NB)]

    def push(offset, half):
        src, dst = ((o_held, o_all), (s_held, s_all))[half]
        return pltpu.make_async_remote_copy(
            src_ref=src.at[offset],
            dst_ref=dst.at[offset],
            send_sem=send.at[offset, half],
            recv_sem=arrive.at[offset, half],
            device_id=(group, peer_at(place, offset)),
            device_id_type=MESH,
        )

    def leave(offset):
        push(offset, 0).start()
        push(offset, 1).start()

    def done(offset):
        push(offset, 0).wait()
        push(offset, 1).wait()

    def pair(dx):
        for offset in range(2):
            head = peer_at(place, 2 * dx + offset)
            lanes = pl.ds(pl.multiple_of(head * HD, HD), HD)
            rows = rows_of(q_ref[2 * dx + offset, slot])
            newer = fresh_scores(nk_ref[slot, :, lanes], rows, table[FIRST])
            older = times(arrived[0, :, :, lanes].reshape(SEG, HD), rows, CONTRACT_LAST)
            older = jnp.concatenate(
                [
                    jnp.where(
                        within < count - starts[j], older[j * BLOCK : (j + 1) * BLOCK], LOWEST
                    )
                    for j in range(NB)
                ]
            )
            top = jnp.maximum(
                jnp.max(older, axis=0, keepdims=True), jnp.max(newer, axis=0, keepdims=True)
            )
            top = jnp.maximum(top, FLOOR)
            old = jnp.exp2((older - top) * FACTOR)
            new = jnp.exp2((newer - top) * FACTOR)
            total = jnp.sum(old, axis=0, keepdims=True) + jnp.sum(new, axis=0, keepdims=True)
            summed = times(
                arrived[1, :, :, lanes].reshape(SEG, HD), old.astype(BF16), CONTRACT_FIRST
            )
            summed += times(nv_ref[slot, :, lanes], new.astype(BF16), CONTRACT_FIRST)
            o_held[2 * dx + offset] = summed.astype(BF16)
            s_held[2 * dx + offset] = stats_of(top, total)

    def onward(dx):
        leave(2 * dx)
        leave(2 * dx + 1)
        pair((dx + 1) % 4)

    pair(1)
    pl.semaphore_wait(barrier, WIDTH - 1)
    in_order(onward, 1, 4)
    leave(1)
    in_order(done, 1, WIDTH)
    o_all[0] = o_held[0]
    s_all[0] = s_held[0]
    _, total, merged = fold(
        WIDTH,
        lambda j: s_all[j, 0:1],
        lambda j: s_all[j, 1:2],
        lambda j: o_all[j].astype(jnp.float32),
    )
    write_rows(out_ref, 0, merged / total)


def close(table, queries, arrived, new_keys, new_values):
    inside = pl.BlockSpec(memory_space=pltpu.VMEM)
    dma = pltpu.SemaphoreType.DMA((WIDTH, 2))
    sums = pltpu.VMEM((WIDTH, HD, ROWS), BF16)
    stats = pltpu.VMEM((WIDTH, 8, ROWS), jnp.float32)
    return pl.pallas_call(
        close_body,
        in_specs=[pl.BlockSpec(memory_space=pltpu.SMEM)] + [inside] * 4,
        out_specs=inside,
        out_shape=jax.ShapeDtypeStruct((1, NEW, GQ * HD), BF16),
        scratch_shapes=[sums, stats, sums, stats, dma, dma],
        compiler_params=pltpu.CompilerParams(collective_id=1, has_side_effects=True),
        cost_estimate=estimate(24 << 20),
        name="close",
    )(table, queries, arrived, new_keys, new_values)


def settle_body(
    table, early, last, arrived, keys_in, values_in, out_ref, keys, values, held, into, outof
):
    def lay(i):
        write_rows(out_ref, table[ORDER + i], early[i])

    put(
        2,
        table,
        arrived,
        keys,
        values,
        held,
        into,
        outof,
        lambda: in_order(lay, 0, SLOTS - 1),
    )
    out_ref[table[ORDER + SLOTS - 1]] = last[0]


def settle(table, early, last, arrived, keys, values):
    inside = pl.BlockSpec(memory_space=pltpu.VMEM)
    sem = pltpu.SemaphoreType.DMA((NB, 2))
    return pl.pallas_call(
        settle_body,
        grid_spec=pltpu.PrefetchScalarGridSpec(
            num_scalar_prefetch=1,
            grid=(),
            in_specs=[inside] * 2 + [ANYWHERE] * 3,
            out_specs=[inside] + [ANYWHERE] * 2,
            scratch_shapes=[HELD, sem, sem],
        ),
        out_shape=[jax.ShapeDtypeStruct((SLOTS, NEW, GQ * HD), BF16), CACHE, CACHE],
        input_output_aliases={4: 1, 5: 2},
        cost_estimate=estimate(8 << 20),
        name="settle",
    )(table, early, last, arrived, keys, values)


def matched(branch, run, *args):
    def at(d):
        route = [(g, g ^ d) for g in range(GROUPS)]
        return functools.partial(run, lambda block: lax.ppermute(block, "group", route))

    return lax.switch(branch.reshape(()), [at(d) for d in range(1, GROUPS)], *args)


def shards(
    query, cache_keys, cache_values, new_keys, new_values, masks, movers, block_lists, lengths
):
    query, keys, values = query[0], cache_keys[0], cache_values[0]
    across = lax.ppermute(query, "ctx", [(c, c ^ 1) for c in range(WIDTH)])
    *branches, table, payload = begin(masks, movers, block_lists, lengths, keys, values)
    new_keys, new_values = new_keys[0], new_values[0]

    def first(permute, table, payload, query, across, keys, values):
        arrived = permute(payload)
        return arrived, gather(query, across), *stage(table, keys, values)

    def second(permute, table, payload, arrived, queries, keys, values, new_keys, new_values):
        now = permute(payload)
        keys, values, ready = renew(table, arrived, keys, values)
        partial = attend(0, 2, 4, table, queries, keys, values, new_keys, new_values)
        return now, ready, keys, values, *partial

    def third(
        permute, table, payload, arrived, queries, keys, values, new_keys, new_values, *partial
    ):
        now = permute(payload)
        keys, values = unpack(1, table, arrived, keys, values)
        partial = attend(
            2, 1, 2, table, queries, keys, values, new_keys, new_values, *partial
        )
        return now, keys, values, reduce(*partial)

    arrived, queries, keys, values, ready = matched(
        branches[0], first, table, payload, query, across, keys, values
    )
    payload = again(1, table, arrived, ready)
    state = (queries, keys, values, new_keys, new_values)
    arrived, ready, keys, values, *partial = matched(
        branches[1], second, table, payload, arrived, *state
    )
    payload = again(2, table, arrived, ready)
    state = (queries, keys, values, new_keys, new_values)
    arrived, keys, values, early = matched(
        branches[2], third, table, payload, arrived, *state, *partial
    )
    last = close(table, queries, arrived, new_keys, new_values)
    attended, keys, values = settle(table, early, last, arrived, keys, values)
    return (attended[None], keys[None], values[None])


def solution(mesh):
    placed = (
        P("group", None, None, "ctx"),
        P("group", None, "ctx", None),
        P("group", None, "ctx", None),
        P("group", None, "ctx", None),
        P("group", None, "ctx", None),
        P(),
        P(),
        P(),
        P(),
    )
    return jax.shard_map(
        shards,
        mesh=mesh,
        in_specs=placed,
        out_specs=(
            P("group", None, None, "ctx"),
            P("group", None, "ctx", None),
            P("group", None, "ctx", None),
        ),
        check_vma=False,
    )
```
